512 devices in a mesh: chan: 64 (over y, z_hi, core), patch: 8 (over x, z_lo).
Axes of the slice: x: 4, y: 8, z: 8 (z_hi: 4, z_lo: 2; z = z_hi * 2 + z_lo), core: 2. Of those that a mesh axis runs over, the one named last changes fastest.
Arguments:
- volume: bfloat16 [8, 2048, 1024], P('patch', 'chan'), may hold values from -6 to 6
- depth_kernel: bfloat16 [27, 2048], P(None, 'chan'), may hold values from -1.25 to 1.25
- mix_weight: bfloat16 [2048, 2048], P('chan'), may hold values from -0.125 to 0.125
- mix_bias: bfloat16 [2048], P('chan'), may hold values from -3 to 3
- out_grad: bfloat16 [8, 2048, 1024], P('patch', 'chan'), may hold values from -1.5 to 1.5
Outputs:
- activated: bfloat16 [8, 2048, 1024], P('patch', 'chan')
- volume_grad: bfloat16 [8, 2048, 1024], P('patch', 'chan')
- kernel_grad: float32 [27, 2048], P(None, 'chan')
- weight_grad: float32 [2048, 2048], P('chan')
- bias_grad: float32 [2048], P('chan')
The draws below stay inside these ranges and needn't reach their ends.
All inputs are finite; a program needn't handle non-finite values.
Results may differ from the reference program's by a relative error of at most 0.011.
Values may be sent and summed in bfloat16 or wider, within the bound.
A program may use at most 64 MiB of HBM per device.

```python
import jax
import jax.numpy as jnp
from jax import lax

C = 2048
DEPTH = 2
ROWS = 16
SIDE = 32
TAPS = 27
CELLS = 1024
PATCHES = 8


def levels(rng, dims, cuts, low, high):
    def one(axis_at, blocks):
        draws = jax.random.uniform(jax.random.fold_in(jax.random.fold_in(rng, 6), axis_at), (blocks,), jnp.float32, low / len(cuts), high / len(cuts))
        return jnp.repeat(jnp.exp(draws), dims[axis_at] // blocks).reshape((-1,) + (1,) * (len(dims) - axis_at - 1))

    loudness = one(*cuts[0])
    for cut in cuts[1:]:
        loudness = loudness * one(*cut)
    return loudness


def normal_values(rng, shape, deviation, bound, shards=(), kind=jnp.bfloat16):
    level = levels(rng, shape, shards, -0.22, 0.18) if shards else 1.0
    result = jax.random.normal(rng, shape, jnp.float32) * deviation * level
    return jnp.minimum(jnp.maximum(result, -bound), bound).astype(kind)


def setup_inputs(seed: int = 0) -> dict:
    arg_keys = jax.random.split(jax.random.key(seed), 6)
    volume = normal_values(arg_keys[0], (PATCHES, C, CELLS), 1.0, 6.0, ((0, 8), (1, 64)))
    depth_kernel = normal_values(arg_keys[1], (TAPS, C), TAPS ** -0.5, 1.25, ((1, 64),))
    mix_weight = normal_values(arg_keys[2], (C, C), C ** -0.5, 0.125, ((0, 64),))
    mix_bias = normal_values(arg_keys[3], (C,), 0.5, 3.0, ((0, 64),))
    out_grad = normal_values(arg_keys[4], (PATCHES, C, CELLS), 0.25, 1.5, ((0, 8), (1, 64)))
    return {"volume": volume, "depth_kernel": depth_kernel, "mix_weight": mix_weight, "mix_bias": mix_bias, "out_grad": out_grad}


def tap_list():
    return [(step_z, step_y, step_x) for step_z in (-1, 0, 1) for step_y in (-1, 0, 1) for step_x in (-1, 0, 1)]


def shifted(values, step_z, step_y, step_x):
    cell_total = DEPTH * ROWS * SIDE
    offset = step_z * ROWS * SIDE + step_y * SIDE + step_x
    margin = ROWS * SIDE + SIDE + 1
    pad_spec = [(0, 0)] * (values.ndim - 1) + [(margin, margin)]
    padded = jnp.pad(values, pad_spec)
    moved_values = lax.slice_in_dim(padded, margin + offset, margin + offset + cell_total, axis=values.ndim - 1)
    cell_index = jnp.arange(cell_total, dtype=jnp.int32)
    cell_plane = cell_index // (ROWS * SIDE)
    cell_row = (cell_index // SIDE) % ROWS
    cell_column = cell_index % SIDE
    inside = (cell_plane + step_z >= 0) & (cell_plane + step_z < DEPTH)
    inside = inside & (cell_row + step_y >= 0) & (cell_row + step_y < ROWS)
    inside = inside & (cell_column + step_x >= 0) & (cell_column + step_x < SIDE)
    return jnp.where(inside, moved_values, jnp.zeros_like(moved_values))


def depthwise(values, kernel, direction_sign):
    total = jnp.zeros_like(values)
    for tap_index, steps in enumerate(tap_list()):
        moved_values = shifted(values, direction_sign * steps[0], direction_sign * steps[1], direction_sign * steps[2])
        total = total + kernel[tap_index][None, :, None] * moved_values
    return total


def reference(volume, depth_kernel, mix_weight, mix_bias, out_grad):
    vol_float = volume.astype(jnp.float32)
    kernel_float = depth_kernel.astype(jnp.float32)
    mixed_in = depthwise(vol_float, kernel_float, 1).astype(jnp.bfloat16)

    def forward_one(inputs):
        return jnp.dot(mix_weight, inputs, preferred_element_type=jnp.float32)

    pre = lax.map(forward_one, mixed_in) + mix_bias.astype(jnp.float32)[None, :, None]
    gate = jax.nn.sigmoid(pre)
    activated = (pre * gate).astype(jnp.bfloat16)
    pre_grad = (out_grad.astype(jnp.float32) * gate * (1.0 + pre * (1.0 - gate))).astype(jnp.bfloat16)

    def weight_one(operands):
        return jnp.dot(operands[0], operands[1].T, preferred_element_type=jnp.float32)

    weight_grad = jnp.sum(lax.map(weight_one, (pre_grad, mixed_in)), axis=0)
    bias_grad = jnp.sum(pre_grad.astype(jnp.float32), axis=(0, 2))

    def backward_one(grads):
        return jnp.dot(mix_weight.T, grads, preferred_element_type=jnp.float32)

    mixed_grad = lax.map(backward_one, pre_grad).astype(jnp.bfloat16)
    grad_float = mixed_grad.astype(jnp.float32)
    volume_grad = depthwise(grad_float, kernel_float, -1).astype(jnp.bfloat16)
    kernel_rows = [jnp.sum(grad_float * shifted(vol_float, steps[0], steps[1], steps[2]), axis=(0, 2)) for steps in tap_list()]
    kernel_grad = jnp.stack(kernel_rows, axis=0)
    return (activated, volume_grad, kernel_grad, weight_grad, bias_grad)
```

```python
import jax
import jax.numpy as jnp
from jax import lax
from jax.experimental import pallas as pl
from jax.experimental.pallas import tpu as pltpu
from jax.sharding import PartitionSpec as P

MESH = pl.DeviceIdType.MESH
F32 = jnp.float32
BF16 = jnp.bfloat16
CELLS = 1024
PLANE = 512
SIDE = 32


def lanes(shape):
    return lax.broadcasted_iota(jnp.int32, shape, len(shape) - 1)


def inside_masks(shape):
    lane = lanes(shape)
    column = lane % SIDE
    row = (lane // SIDE) % 16
    return {
        ("c", 1): column < SIDE - 1,
        ("c", -1): column > 0,
        ("r", 1): row < 15,
        ("r", -1): row > 0,
    }


def moved(values, masks, kind, step):
    if step == 0:
        return values
    amount = step * (1 if kind == "c" else SIDE)
    rolled = pltpu.roll(values, (-amount) % CELLS, 1)
    return jnp.where(masks[(kind, step)], rolled, 0.0)


def tap(a, b, c):
    return 9 * (a + 1) + 3 * (b + 1) + (c + 1)


def kernel(
    vol_ref, dk_ref, w_ref, bias_ref, og_ref,
    act_ref, vg_ref, kb_ref, wg_ref,
    mst, ogs, g_buf, ogb, wb, wt, pg_ref, apst, apb, pmb, pmr, mgs, mgr,
    sbs, sbr, cs, xb, xr, zb, zr, fb, kbs,
    m_s, m_r, o_s, o_r, wz_s, wz_r, wx_s, wx_r, wc_s, wc_r, y_s, y_r, ry_s, ry_r, ap_s, ap_r,
    c_s, c_r, x_s, x_r, z_s, z_r, f_s, f_r, b_s, b_r, k_s, k_r,
):
    chan = lax.axis_index("chan")
    patch = lax.axis_index("patch")
    y, i = chan // 8, chan % 8
    zh, core = i // 2, i % 2
    x, zl = patch // 2, patch % 2
    zz = zh * 2 + zl
    oi = core * 4 + zh
    other = 1 - core

    def at_i(k):
        return (y * 8 + (i + k) % 8, patch)

    def at_y(k):
        return (((y + k) % 8) * 8 + i, patch)

    def at_x(k):
        return (chan, ((x + k) % 4) * 2 + zl)

    def at_p(k):
        return (chan, (patch + k) % 8)

    def at_z(k):
        to = (zz + k) % 8
        return (y * 8 + (to // 2) * 2 + core, x * 2 + to % 2)

    def at_zh(k):
        return (y * 8 + ((zh + k) % 4) * 2 + core, patch)

    sibling = (y * 8 + zh * 2 + other, patch)

    pending = []

    def send(src, dst, ssem, rsem, where):
        copy = pltpu.make_async_remote_copy(
            src_ref=src, dst_ref=dst, send_sem=ssem, recv_sem=rsem, device_id=where, device_id_type=MESH
        )
        copy.start()
        pending.append(copy)

    def arrive(dst, ssem, rsem, where):
        pltpu.make_async_remote_copy(
            src_ref=dst, dst_ref=dst, send_sem=ssem, recv_sem=rsem, device_id=where, device_id_type=MESH
        ).wait_recv()

    barrier = pltpu.get_barrier_semaphore()
    peers = [at_i(k) for k in range(1, 8)] + [at_y(k) for k in range(1, 8)] + [at_p(k) for k in range(1, 8)]
    peers += [
        (y * 8 + ((zh + k) % 4) * 2 + core, x * 2 + (1 - zl)) for k in range(1, 4)
    ]
    for peer in peers:
        pl.semaphore_signal(barrier, inc=1, device_id=peer, device_id_type=MESH)

    eye = (
        lax.broadcasted_iota(jnp.int32, (27, 128), 0) == lax.broadcasted_iota(jnp.int32, (27, 128), 1)
    ).astype(F32).astype(BF16)
    taps = lax.dot_general(dk_ref[...], eye, (((0,), (0,)), ((), ())), preferred_element_type=F32)

    masks = inside_masks((8, CELLS))
    for g in range(4):
        rows = slice(8 * g, 8 * g + 8)
        v = vol_ref[0, rows, :].astype(F32)
        vc = {c: moved(v, masks, "c", c) for c in (-1, 0, 1)}
        total = None
        for b in (-1, 0, 1):
            def mixed(a, plane):
                part = slice(plane * PLANE, plane * PLANE + PLANE)
                out = None
                for c in (-1, 0, 1):
                    t = tap(a, b, c)
                    term = taps[rows, t : t + 1] * vc[c][:, part]
                    out = term if out is None else out + term
                return out

            first = mixed(0, 0) + mixed(1, 1)
            second = mixed(0, 1) + mixed(-1, 0)
            part = moved(jnp.concatenate([first, second], axis=1), masks, "r", b)
            total = part if total is None else total + part
        for k in range(8):
            mst[k, rows, :] = total[:, 128 * k : 128 * k + 128].astype(BF16)

    pl.semaphore_wait(barrier, len(peers))

    for k in range(1, 8):
        to = (i + k) % 8
        send(mst.at[to], g_buf.at[y, i], m_s.at[k], m_r.at[k], at_i(k))
    quarter = pl.ds(pl.multiple_of(x * 512, 512), 512)
    for k in range(1, 4):
        send(w_ref.at[:, quarter], wb.at[x, core, zh], wz_s.at[k], wz_r.at[k], at_zh(k))
    wb[x, core, zh] = w_ref[:, quarter]
    g_buf[y, i] = mst[i]

    diag = lax.broadcasted_iota(jnp.int32, (32, 32), 0) == lax.broadcasted_iota(jnp.int32, (32, 32), 1)
    spread = jnp.where(diag, jnp.broadcast_to(bias_ref[...].astype(F32), (32, 32)), 0.0).astype(BF16)
    bias = jnp.dot(spread, jnp.ones((32, 128), BF16), preferred_element_type=F32).astype(BF16)
    for k in range(8):
        ogs[k, 0] = og_ref[0, :, 128 * k : 128 * k + 128]
        ogs[k, 1] = bias

    for k in range(1, 8):
        arrive(g_buf.at[y, (i - k) % 8], m_s.at[k], m_r.at[k], at_i(k))
    for k in (4, 3, 5, 2, 6, 1, 7):
        send(g_buf.at[y], g_buf.at[y], y_s.at[k], y_r.at[k], at_y(k))

    for k in range(1, 8):
        to = (i + k) % 8
        send(ogs.at[to], ogb.at[oi], o_s.at[k], o_r.at[k], at_i(k))
    ogb[oi] = ogs[i]

    for k in range(1, 4):
        arrive(wb.at[x, core, (zh - k) % 4], wz_s.at[k], wz_r.at[k], at_zh(k))
    for k in range(1, 4):
        send(wb.at[x, core], wb.at[x, core], wx_s.at[k], wx_r.at[k], at_x(k))
    send(wb.at[x, core], wb.at[x, core], wc_s.at[0], wc_r.at[0], sibling)
    for k in (1, 3, 2):
        q = (x - k) % 4
        arrive(wb.at[q, core], wx_s.at[k], wx_r.at[k], at_x(k))
        send(wb.at[q, core], wb.at[q, core], wc_s.at[k], wc_r.at[k], sibling)
    for k in range(4):
        arrive(wb.at[(x - k) % 4, other], wc_s.at[k], wc_r.at[k], sibling)

    for q in range(4):
        block = wb[q].reshape(256, 512)
        for h in range(2):
            wt[2 * q + h] = block[:, 256 * h : 256 * h + 256].T

    for k in range(1, 8):
        arrive(ogb.at[(((i - k) % 8) % 2) * 4 + ((i - k) % 8) // 2], o_s.at[k], o_r.at[k], at_i(k))

    for k in range(1, 8):
        arrive(g_buf.at[(y - k) % 8], y_s.at[k], y_r.at[k], at_y(k))

    pre = ogb[:, 1].reshape(256, 128).astype(F32)
    for q in range(4):
        pre = pre + jnp.dot(
            wb[q].reshape(256, 512), g_buf[2 * q : 2 * q + 2].reshape(512, 128), preferred_element_type=F32
        )
    gate = jax.nn.sigmoid(pre)
    pre_grad = (ogb[:, 0].reshape(256, 128).astype(F32) * gate * (1.0 + pre * (1.0 - gate))).astype(BF16)
    pg_ref[...] = pre_grad.reshape(2, 128, 128)

    for k in (4, 3, 5, 2, 6, 1, 7):
        to = (y + k) % 8
        pmb[k] = jnp.dot(wt[to], pre_grad, preferred_element_type=F32).astype(BF16)
        send(pmb.at[k], pmr.at[k], ry_s.at[k], ry_r.at[k], at_y(k))

    theirs = pg_ref[other]
    for q in range(4):
        sbs[q] = lax.dot_general(
            theirs, g_buf[2 * q : 2 * q + 2].reshape(512, 128), (((1,), (1,)), ((), ())), preferred_element_type=F32
        ).astype(BF16)
    send(sbs, sbr, c_s.at[0], c_r.at[0], sibling)

    activated = (pre * gate).astype(BF16)
    apst[:, 0] = activated.reshape(8, 32, 128)
    apst[:, 1] = pre_grad.reshape(8, 32, 128)
    for k in range(1, 8):
        to = (i + k) % 8
        send(apst.at[(to % 2) * 4 + to // 2], apb.at[i], ap_s.at[k], ap_r.at[k], at_i(k))
    apb[i] = apst[oi]

    mine = pg_ref[core]
    for q in range(4):
        cs[q] = lax.dot_general(
            mine, g_buf[2 * q : 2 * q + 2].reshape(512, 128), (((1,), (1,)), ((), ())), preferred_element_type=F32
        )
    own = jnp.dot(wt[y], pre_grad, preferred_element_type=F32)

    arrive(sbr, c_s.at[0], c_r.at[0], sibling)
    for k in (2, 1, 3):
        to = (x + k) % 4
        xb[k] = (cs[to] + sbr[to].astype(F32)).astype(BF16)
        send(xb.at[k], xr.at[k], x_s.at[k], x_r.at[k], at_x(k))
    cs[x] = cs[x] + sbr[x].astype(F32)

    for k in range(1, 8):
        arrive(apb.at[(i - k) % 8], ap_s.at[k], ap_r.at[k], at_i(k))
    bias_sum = None
    for k in range(8):
        act_ref[0, :, 128 * k : 128 * k + 128] = apb[k, 0]
        part = apb[k, 1].astype(F32)
        bias_sum = part if bias_sum is None else bias_sum + part
    bias_sum = jnp.sum(bias_sum, axis=1, keepdims=True)

    for k in range(1, 4):
        arrive(xr.at[k], x_s.at[k], x_r.at[k], at_x(k))
    summed = cs[x] + xr[1].astype(F32) + xr[2].astype(F32) + xr[3].astype(F32)
    for h in range(4):
        for l in range(2):
            zb[2 * h + l] = summed[32 * h : 32 * h + 32, 256 * l : 256 * l + 256].astype(BF16)
    for k in range(1, 8):
        to = (zz + k) % 8
        send(zb.at[to], zr.at[k], z_s.at[k], z_r.at[k], at_z(k))

    for k in range(1, 8):
        arrive(pmr.at[k], ry_s.at[k], ry_r.at[k], at_y(k))
    for k in range(1, 8):
        own = own + pmr[k].astype(F32)
    mgs[...] = own.astype(BF16).reshape(8, 32, 128)
    for k in range(1, 8):
        to = (i + k) % 8
        send(mgs.at[to], mgr.at[i], b_s.at[k], b_r.at[k], at_i(k))
    mgr[i] = mgs[i]

    for k in range(1, 8):
        arrive(zr.at[k], z_s.at[k], z_r.at[k], at_z(k))
    final = zb[zz].astype(F32)
    for k in range(1, 8):
        final = final + zr[k].astype(F32)
    fb[patch] = final
    for k in range(1, 8):
        send(fb.at[patch], fb.at[patch], f_s.at[k], f_r.at[k], at_p(k))

    for k in range(1, 8):
        arrive(mgr.at[(i - k) % 8], b_s.at[k], b_r.at[k], at_i(k))

    lane = lanes((8, 128))
    for g in range(4):
        rows = slice(8 * g, 8 * g + 8)
        v = vol_ref[0, rows, :].astype(F32)
        grad = jnp.concatenate([mgr[k, rows, :].astype(F32) for k in range(8)], axis=1)
        v0, v1 = v[:, :PLANE], v[:, PLANE:]
        out0 = jnp.zeros((8, PLANE), F32)
        out1 = jnp.zeros((8, PLANE), F32)
        tile = jnp.where(lane == 27, bias_sum[rows, :], 0.0)
        for b in (-1, 0, 1):
            row_moved = moved(grad, masks, "r", -b)
            for c in (-1, 0, 1):
                gm = moved(row_moved, masks, "c", -c)
                g0, g1 = gm[:, :PLANE], gm[:, PLANE:]
                tm, tz, tp = tap(-1, b, c), tap(0, b, c), tap(1, b, c)
                out0 = out0 + taps[rows, tz : tz + 1] * g0 + taps[rows, tm : tm + 1] * g1
                out1 = out1 + taps[rows, tz : tz + 1] * g1 + taps[rows, tp : tp + 1] * g0
                for t, product in ((tm, v0 * g1), (tz, v0 * g0 + v1 * g1), (tp, v1 * g0)):
                    tile = jnp.where(lane == t, jnp.sum(product, axis=1, keepdims=True), tile)
        vg_ref[0, rows, :PLANE] = out0.astype(BF16)
        vg_ref[0, rows, PLANE:] = out1.astype(BF16)
        kbs[patch, rows, :] = tile
    for k in range(1, 8):
        send(kbs.at[patch], kbs.at[patch], k_s.at[k], k_r.at[k], at_p(k))

    for k in range(1, 8):
        arrive(fb.at[(patch - k) % 8], f_s.at[k], f_r.at[k], at_p(k))
    for k in range(8):
        wg_ref[:, 256 * k : 256 * k + 256] = fb[k]
    for k in range(1, 8):
        arrive(kbs.at[(patch - k) % 8], k_s.at[k], k_r.at[k], at_p(k))
    kb = kbs[0]
    for k in range(1, 8):
        kb = kb + kbs[k]
    kb_ref[...] = kb
    for copy in pending:
        copy.wait_send()


def body(volume, depth_kernel, mix_weight, mix_bias, out_grad):
    vmem = pl.BlockSpec(memory_space=pltpu.VMEM)
    sem = pltpu.SemaphoreType.DMA
    act, vg, kb, wg = pl.pallas_call(
        kernel,
        out_shape=(
            jax.ShapeDtypeStruct((1, 32, CELLS), BF16),
            jax.ShapeDtypeStruct((1, 32, CELLS), BF16),
            jax.ShapeDtypeStruct((32, 128), F32),
            jax.ShapeDtypeStruct((32, 2048), F32),
        ),
        in_specs=[vmem] * 5,
        out_specs=(vmem,) * 4,
        scratch_shapes=[
            pltpu.VMEM((8, 32, 128), BF16),
            pltpu.VMEM((8, 2, 32, 128), BF16),
            pltpu.VMEM((8, 8, 32, 128), BF16),
            pltpu.VMEM((8, 2, 32, 128), BF16),
            pltpu.VMEM((4, 2, 4, 32, 512), BF16),
            pltpu.VMEM((8, 256, 256), BF16),
            pltpu.VMEM((2, 128, 128), BF16),
            pltpu.VMEM((8, 2, 32, 128), BF16),
            pltpu.VMEM((8, 2, 32, 128), BF16),
            pltpu.VMEM((8, 256, 128), BF16),
            pltpu.VMEM((8, 256, 128), BF16),
            pltpu.VMEM((8, 32, 128), BF16),
            pltpu.VMEM((8, 32, 128), BF16),
            pltpu.VMEM((4, 128, 512), BF16),
            pltpu.VMEM((4, 128, 512), BF16),
            pltpu.VMEM((4, 128, 512), F32),
            pltpu.VMEM((4, 128, 512), BF16),
            pltpu.VMEM((4, 128, 512), BF16),
            pltpu.VMEM((8, 32, 256), BF16),
            pltpu.VMEM((8, 32, 256), BF16),
            pltpu.VMEM((8, 32, 256), F32),
            pltpu.VMEM((8, 32, 128), F32),
            sem((8,)), sem((8,)), sem((8,)), sem((8,)),
            sem((4,)), sem((4,)), sem((4,)), sem((4,)), sem((4,)), sem((4,)),
            sem((8,)), sem((8,)), sem((8,)), sem((8,)), sem((8,)), sem((8,)),
            sem((1,)), sem((1,)), sem((4,)), sem((4,)), sem((8,)), sem((8,)),
            sem((8,)), sem((8,)), sem((8,)), sem((8,)), sem((8,)), sem((8,)),
        ],
        compiler_params=pltpu.CompilerParams(
            collective_id=0, has_side_effects=True, vmem_limit_bytes=40 * 1024 * 1024
        ),
    )(volume, depth_kernel, mix_weight, mix_bias.reshape(1, 32), out_grad)
    return act, vg, kb[:, :27].T, wg, kb[:, 27]


def solution(mesh):
    placed = (
        P("patch", "chan", None),
        P(None, "chan"),
        P("chan", None),
        P("chan"),
        P("patch", "chan", None),
    )
    return jax.shard_map(
        body,
        mesh=mesh,
        in_specs=placed,
        out_specs=(
            P("patch", "chan", None),
            P("patch", "chan", None),
            P(None, "chan"),
            P("chan", None),
            P("chan"),
        ),
        check_vma=False,
    )
```

```python
import jax
import jax.numpy as jnp
from jax import lax
from jax.experimental import pallas as pl
from jax.experimental.pallas import tpu as pltpu
from jax.sharding import PartitionSpec as P

MESH = pl.DeviceIdType.MESH
F32 = jnp.float32
BF16 = jnp.bfloat16
CELLS = 1024
PLANE = 512
SIDE = 32


def lanes(shape):
    return lax.broadcasted_iota(jnp.int32, shape, len(shape) - 1)


def inside_masks(shape):
    lane = lanes(shape)
    column = lane % SIDE
    row = (lane // SIDE) % 16
    return {
        ("c", 1): column < SIDE - 1,
        ("c", -1): column > 0,
        ("r", 1): row < 15,
        ("r", -1): row > 0,
    }


def moved(values, masks, kind, step):
    if step == 0:
        return values
    amount = step * (1 if kind == "c" else SIDE)
    rolled = pltpu.roll(values, (-amount) % CELLS, 1)
    return jnp.where(masks[(kind, step)], rolled, 0.0)


def tap(a, b, c):
    return 9 * (a + 1) + 3 * (b + 1) + (c + 1)


def kernel(
    vol_hbm, dk_hbm, w_hbm, bias_hbm, og_hbm,
    act_ref, vg_ref, kg_ref, wg_ref, bg_ref,
    vol_ref, dk_ref, w_ref, bias_ref, og_ref, in_sem,
    mst, ogs, g_buf, ogb, wb, wt, pg_ref, apst, apb, pm, r1, r2, r3, r4, mid, mgs, mgr,
    sbs, sbr, cs, xb, xr, zb, zr, fb, kbs,
    m_s, m_r, o_s, o_r, wz_s, wz_r, wx_s, wx_r, wc_s, wc_r, y_s, y_r, ry_s, ry_r, ap_s, ap_r,
    c_s, c_r, x_s, x_r, z_s, z_r, f_s, f_r, b_s, b_r, k_s, k_r,
):
    chan = lax.axis_index("chan")
    patch = lax.axis_index("patch")
    y, i = chan // 8, chan % 8
    zh, core = i // 2, i % 2
    x, zl = patch // 2, patch % 2
    zz = zh * 2 + zl
    oi = core * 4 + zh
    other = 1 - core

    def at_i(k):
        return (y * 8 + (i + k) % 8, patch)

    def at_y(k):
        return (((y + k) % 8) * 8 + i, patch)

    def at_x(k):
        return (chan, ((x + k) % 4) * 2 + zl)

    def at_p(k):
        return (chan, (patch + k) % 8)

    def at_z(k):
        to = (zz + k) % 8
        return (y * 8 + (to // 2) * 2 + core, x * 2 + to % 2)

    def at_zh(k):
        return (y * 8 + ((zh + k) % 4) * 2 + core, patch)

    sibling = (y * 8 + zh * 2 + other, patch)

    pending = []

    def send(src, dst, ssem, rsem, where):
        copy = pltpu.make_async_remote_copy(
            src_ref=src, dst_ref=dst, send_sem=ssem, recv_sem=rsem, device_id=where, device_id_type=MESH
        )
        copy.start()
        pending.append(copy)

    def arrive(dst, ssem, rsem, where):
        pltpu.make_async_remote_copy(
            src_ref=dst, dst_ref=dst, send_sem=ssem, recv_sem=rsem, device_id=where, device_id_type=MESH
        ).wait_recv()

    barrier = pltpu.get_barrier_semaphore()
    peers = [at_i(k) for k in range(1, 8)] + [at_y(k) for k in (1, 2, 6, 7)] + [at_p(k) for k in range(1, 8)]
    peers += [
        (y * 8 + ((zh + k) % 4) * 2 + core, x * 2 + (1 - zl)) for k in range(1, 4)
    ]
    for peer in peers:
        pl.semaphore_signal(barrier, inc=1, device_id=peer, device_id_type=MESH)

    loads = [
        pltpu.make_async_copy(src, dst, in_sem.at[n])
        for n, (src, dst) in enumerate(
            [(vol_hbm, vol_ref), (dk_hbm, dk_ref), (w_hbm, w_ref), (bias_hbm, bias_ref), (og_hbm, og_ref)]
        )
    ]
    for load in loads:
        load.start()
    loads[1].wait()
    loads[0].wait()

    eye = (
        lax.broadcasted_iota(jnp.int32, (27, 128), 0) == lax.broadcasted_iota(jnp.int32, (27, 128), 1)
    ).astype(F32).astype(BF16)
    taps = lax.dot_general(dk_ref[...], eye, (((0,), (0,)), ((), ())), preferred_element_type=F32)

    masks = inside_masks((8, CELLS))
    for g in range(4):
        rows = slice(8 * g, 8 * g + 8)
        v = vol_ref[0, rows, :].astype(F32)
        vc = {c: moved(v, masks, "c", c) for c in (-1, 0, 1)}
        total = None
        for b in (-1, 0, 1):
            def mixed(a, plane):
                part = slice(plane * PLANE, plane * PLANE + PLANE)
                out = None
                for c in (-1, 0, 1):
                    t = tap(a, b, c)
                    term = taps[rows, t : t + 1] * vc[c][:, part]
                    out = term if out is None else out + term
                return out

            first = mixed(0, 0) + mixed(1, 1)
            second = mixed(0, 1) + mixed(-1, 0)
            part = moved(jnp.concatenate([first, second], axis=1), masks, "r", b)
            total = part if total is None else total + part
        for k in range(8):
            mst[k, rows, :] = total[:, 128 * k : 128 * k + 128].astype(BF16)

    pl.semaphore_wait(barrier, len(peers))

    for k in range(1, 8):
        to = (i + k) % 8
        send(mst.at[to], g_buf.at[y, i], m_s.at[k], m_r.at[k], at_i(k))
    loads[2].wait()
    quarter = pl.ds(pl.multiple_of(x * 512, 512), 512)
    for k in range(1, 4):
        send(w_ref.at[:, quarter], wb.at[x, core, zh], wz_s.at[k], wz_r.at[k], at_zh(k))
    wb[x, core, zh] = w_ref[:, quarter]
    g_buf[y, i] = mst[i]

    loads[3].wait()
    loads[4].wait()
    diag = lax.broadcasted_iota(jnp.int32, (32, 32), 0) == lax.broadcasted_iota(jnp.int32, (32, 32), 1)
    spread = jnp.where(diag, jnp.broadcast_to(bias_ref[...].astype(F32), (32, 32)), 0.0).astype(BF16)
    bias = jnp.dot(spread, jnp.ones((32, 128), BF16), preferred_element_type=F32).astype(BF16)
    for k in range(8):
        ogs[k, 0] = og_ref[0, :, 128 * k : 128 * k + 128]
        ogs[k, 1] = bias

    for k in range(1, 8):
        arrive(g_buf.at[y, (i - k) % 8], m_s.at[k], m_r.at[k], at_i(k))
    low, high = pl.ds(0, 4), pl.ds(4, 4)

    def block(k, half):
        return g_buf.at[(y + k) % 8, half]

    def pass_on(k, half, n, to):
        send(block(k, half), block(k, half), y_s.at[n], y_r.at[n], at_y(to))

    pass_on(0, low, 2, 2)
    pass_on(0, high, 5, 6)
    pass_on(0, high, 3, 2)
    pass_on(0, low, 4, 6)
    whole = pl.ds(0, 8)
    pass_on(0, whole, 0, 1)
    pass_on(0, whole, 1, 7)

    for k in range(1, 8):
        to = (i + k) % 8
        send(ogs.at[to], ogb.at[oi], o_s.at[k], o_r.at[k], at_i(k))
    ogb[oi] = ogs[i]

    for k in range(1, 4):
        arrive(wb.at[x, core, (zh - k) % 4], wz_s.at[k], wz_r.at[k], at_zh(k))
    for k in range(1, 4):
        send(wb.at[x, core], wb.at[x, core], wx_s.at[k], wx_r.at[k], at_x(k))
    send(wb.at[x, core], wb.at[x, core], wc_s.at[0], wc_r.at[0], sibling)

    arrive(block(-2, low), y_s.at[2], y_r.at[2], at_y(2))
    pass_on(-2, low, 8, 2)
    pass_on(-2, low, 6, 1)
    arrive(block(2, high), y_s.at[5], y_r.at[5], at_y(6))
    pass_on(2, high, 11, 6)
    pass_on(2, high, 10, 7)
    arrive(block(-2, high), y_s.at[3], y_r.at[3], at_y(2))
    pass_on(-2, high, 7, 1)
    arrive(block(2, low), y_s.at[4], y_r.at[4], at_y(6))
    pass_on(2, low, 9, 7)

    for k in (1, 3, 2):
        q = (x - k) % 4
        arrive(wb.at[q, core], wx_s.at[k], wx_r.at[k], at_x(k))
        send(wb.at[q, core], wb.at[q, core], wc_s.at[k], wc_r.at[k], sibling)
    for k in (0, 1, 3, 2):
        q = (x - k) % 4
        arrive(wb.at[q, other], wc_s.at[k], wc_r.at[k], sibling)
        part = wb[q].reshape(256, 512)
        for h in range(2):
            wt[2 * q + h] = part[:, 256 * h : 256 * h + 256].T

    for k in range(1, 8):
        arrive(ogb.at[(((i - k) % 8) % 2) * 4 + ((i - k) % 8) // 2], o_s.at[k], o_r.at[k], at_i(k))

    arrive(block(-1, whole), y_s.at[0], y_r.at[0], at_y(1))
    arrive(block(1, whole), y_s.at[1], y_r.at[1], at_y(7))
    arrive(block(-3, low), y_s.at[6], y_r.at[6], at_y(1))
    arrive(block(-3, high), y_s.at[7], y_r.at[7], at_y(1))
    arrive(block(3, low), y_s.at[9], y_r.at[9], at_y(7))
    arrive(block(3, high), y_s.at[10], y_r.at[10], at_y(7))
    arrive(block(4, low), y_s.at[8], y_r.at[8], at_y(2))
    arrive(block(4, high), y_s.at[11], y_r.at[11], at_y(6))

    pre = ogb[:, 1].reshape(256, 128).astype(F32)
    for q in range(4):
        pre = pre + jnp.dot(
            wb[q].reshape(256, 512), g_buf[2 * q : 2 * q + 2].reshape(512, 128), preferred_element_type=F32
        )
    gate = jax.nn.sigmoid(pre)
    pre_grad = (ogb[:, 0].reshape(256, 128).astype(F32) * gate * (1.0 + pre * (1.0 - gate))).astype(BF16)
    pg_ref[...] = pre_grad.reshape(2, 128, 128)

    def partial(k):
        return jnp.dot(wt[(y + k) % 8], pre_grad, preferred_element_type=F32)

    pm[0] = partial(4).astype(BF16)
    send(pm.at[0, pl.ds(0, 128)], r4.at[0], ry_s.at[0], ry_r.at[0], at_y(6))
    send(pm.at[0, pl.ds(128, 128)], r4.at[1], ry_s.at[1], ry_r.at[1], at_y(2))
    pm[1] = partial(-3).astype(BF16)
    send(pm.at[1], r3.at[0], ry_s.at[2], ry_r.at[2], at_y(7))
    pm[2] = partial(3).astype(BF16)
    send(pm.at[2], r3.at[1], ry_s.at[3], ry_r.at[3], at_y(1))
    pm[3] = partial(-1).astype(BF16)
    send(pm.at[3], r1.at[0], ry_s.at[4], ry_r.at[4], at_y(7))
    pm[4] = partial(1).astype(BF16)
    send(pm.at[4], r1.at[1], ry_s.at[5], ry_r.at[5], at_y(1))
    mid[0] = partial(-2)
    mid[1] = partial(2)

    theirs = pg_ref[other]
    for q in range(4):
        sbs[q] = lax.dot_general(
            theirs, g_buf[2 * q : 2 * q + 2].reshape(512, 128), (((1,), (1,)), ((), ())), preferred_element_type=F32
        ).astype(BF16)
    send(sbs, sbr, c_s.at[0], c_r.at[0], sibling)

    activated = (pre * gate).astype(BF16)
    apst[:, 0] = activated.reshape(8, 32, 128)
    apst[:, 1] = pre_grad.reshape(8, 32, 128)
    for k in range(1, 8):
        to = (i + k) % 8
        send(apst.at[(to % 2) * 4 + to // 2], apb.at[i], ap_s.at[k], ap_r.at[k], at_i(k))
    apb[i] = apst[oi]

    mine = pg_ref[core]
    for q in range(4):
        cs[q] = lax.dot_general(
            mine, g_buf[2 * q : 2 * q + 2].reshape(512, 128), (((1,), (1,)), ((), ())), preferred_element_type=F32
        )
    own = partial(0)

    arrive(sbr, c_s.at[0], c_r.at[0], sibling)
    for k in (2, 1, 3):
        to = (x + k) % 4
        xb[k] = (cs[to] + sbr[to].astype(F32)).astype(BF16)
        send(xb.at[k], xr.at[k], x_s.at[k], x_r.at[k], at_x(k))
    cs[x] = cs[x] + sbr[x].astype(F32)

    arrive(r4.at[0], ry_s.at[0], ry_r.at[0], at_y(6))
    arrive(r3.at[0], ry_s.at[2], ry_r.at[2], at_y(7))
    pm[5, :128] = (mid[0, :128] + r3[0, :128].astype(F32) + r4[0].astype(F32)).astype(BF16)
    pm[5, 128:] = (mid[0, 128:] + r3[0, 128:].astype(F32)).astype(BF16)
    send(pm.at[5], r2.at[0], ry_s.at[6], ry_r.at[6], at_y(6))
    arrive(r4.at[1], ry_s.at[1], ry_r.at[1], at_y(2))
    arrive(r3.at[1], ry_s.at[3], ry_r.at[3], at_y(1))
    pm[6, :128] = (mid[1, :128] + r3[1, :128].astype(F32)).astype(BF16)
    pm[6, 128:] = (mid[1, 128:] + r3[1, 128:].astype(F32) + r4[1].astype(F32)).astype(BF16)
    send(pm.at[6], r2.at[1], ry_s.at[7], ry_r.at[7], at_y(2))

    for k in range(1, 8):
        arrive(apb.at[(i - k) % 8], ap_s.at[k], ap_r.at[k], at_i(k))
    bias_sum = None
    for k in range(8):
        act_ref[0, :, 128 * k : 128 * k + 128] = apb[k, 0]
        part = apb[k, 1].astype(F32)
        bias_sum = part if bias_sum is None else bias_sum + part
    bias_sum = jnp.sum(bias_sum, axis=1, keepdims=True)

    arrive(r1.at[0], ry_s.at[4], ry_r.at[4], at_y(7))
    arrive(r1.at[1], ry_s.at[5], ry_r.at[5], at_y(1))
    own = own + r1[0].astype(F32) + r1[1].astype(F32)
    arrive(r2.at[0], ry_s.at[6], ry_r.at[6], at_y(6))
    arrive(r2.at[1], ry_s.at[7], ry_r.at[7], at_y(2))
    own = own + r2[0].astype(F32) + r2[1].astype(F32)
    mgs[...] = own.astype(BF16).reshape(8, 32, 128)
    for k in range(1, 8):
        to = (i + k) % 8
        send(mgs.at[to], mgr.at[i], b_s.at[k], b_r.at[k], at_i(k))
    mgr[i] = mgs[i]

    for k in range(1, 4):
        arrive(xr.at[k], x_s.at[k], x_r.at[k], at_x(k))
    summed = cs[x] + xr[1].astype(F32) + xr[2].astype(F32) + xr[3].astype(F32)
    for h in range(4):
        for l in range(2):
            zb[2 * h + l] = summed[32 * h : 32 * h + 32, 256 * l : 256 * l + 256].astype(BF16)
    for k in range(1, 8):
        to = (zz + k) % 8
        send(zb.at[to], zr.at[k], z_s.at[k], z_r.at[k], at_z(k))

    for k in range(1, 8):
        arrive(mgr.at[(i - k) % 8], b_s.at[k], b_r.at[k], at_i(k))

    lane = lanes((8, 128))
    for g in range(4):
        rows = slice(8 * g, 8 * g + 8)
        v = vol_ref[0, rows, :].astype(F32)
        grad = jnp.concatenate([mgr[k, rows, :].astype(F32) for k in range(8)], axis=1)
        v0, v1 = v[:, :PLANE], v[:, PLANE:]
        out0 = jnp.zeros((8, PLANE), F32)
        out1 = jnp.zeros((8, PLANE), F32)
        tile = jnp.where(lane == 27, bias_sum[rows, :], 0.0)
        for b in (-1, 0, 1):
            row_moved = moved(grad, masks, "r", -b)
            for c in (-1, 0, 1):
                gm = moved(row_moved, masks, "c", -c)
                g0, g1 = gm[:, :PLANE], gm[:, PLANE:]
                tm, tz, tp = tap(-1, b, c), tap(0, b, c), tap(1, b, c)
                out0 = out0 + taps[rows, tz : tz + 1] * g0 + taps[rows, tm : tm + 1] * g1
                out1 = out1 + taps[rows, tz : tz + 1] * g1 + taps[rows, tp : tp + 1] * g0
                for t, product in ((tm, v0 * g1), (tz, v0 * g0 + v1 * g1), (tp, v1 * g0)):
                    tile = jnp.where(lane == t, jnp.sum(product, axis=1, keepdims=True), tile)
        vg_ref[0, rows, :PLANE] = out0.astype(BF16)
        vg_ref[0, rows, PLANE:] = out1.astype(BF16)
        kbs[patch, rows, :] = tile
    for k in range(1, 8):
        send(kbs.at[patch], kbs.at[patch], k_s.at[k], k_r.at[k], at_p(k))

    for k in range(1, 8):
        arrive(zr.at[k], z_s.at[k], z_r.at[k], at_z(k))
    final = zb[zz].astype(F32)
    for k in range(1, 8):
        final = final + zr[k].astype(F32)
    fb[patch] = final.astype(BF16)
    for k in range(1, 8):
        send(fb.at[patch], fb.at[patch], f_s.at[k], f_r.at[k], at_p(k))

    for k in range(1, 8):
        arrive(fb.at[(patch - k) % 8], f_s.at[k], f_r.at[k], at_p(k))
    for k in range(8):
        wg_ref[:, 256 * k : 256 * k + 256] = fb[k].astype(F32)
    for k in range(1, 8):
        arrive(kbs.at[(patch - k) % 8], k_s.at[k], k_r.at[k], at_p(k))
    kb = kbs[0]
    for k in range(1, 8):
        kb = kb + kbs[k]
    turned = kb.T
    kg_ref[...] = turned[:27, :]
    bg_ref[...] = turned[27:28, :]
    for copy in pending:
        copy.wait_send()


def finish_kernel(*refs):
    sources, results, sems = refs[:5], refs[5:10], refs[10]
    copies = [pltpu.make_async_copy(a, b, sems.at[n]) for n, (a, b) in enumerate(zip(sources, results))]
    for copy in copies:
        copy.start()
    for copy in copies:
        copy.wait()


def body(volume, depth_kernel, mix_weight, mix_bias, out_grad):
    vmem = pl.BlockSpec(memory_space=pltpu.VMEM)
    hbm = pl.BlockSpec(memory_space=pltpu.HBM)
    sem = pltpu.SemaphoreType.DMA
    shapes = (
        jax.ShapeDtypeStruct((1, 32, CELLS), BF16),
        jax.ShapeDtypeStruct((1, 32, CELLS), BF16),
        jax.ShapeDtypeStruct((27, 32), F32),
        jax.ShapeDtypeStruct((32, 2048), F32),
        jax.ShapeDtypeStruct((1, 32), F32),
    )
    results = pl.pallas_call(
        kernel,
        out_shape=shapes,
        in_specs=[hbm] * 5,
        out_specs=(vmem,) * 5,
        scratch_shapes=[
            pltpu.VMEM((1, 32, CELLS), BF16),
            pltpu.VMEM((27, 32), BF16),
            pltpu.VMEM((32, 2048), BF16),
            pltpu.VMEM((1, 32), BF16),
            pltpu.VMEM((1, 32, CELLS), BF16),
            sem((5,)),
            pltpu.VMEM((8, 32, 128), BF16),
            pltpu.VMEM((8, 2, 32, 128), BF16),
            pltpu.VMEM((8, 8, 32, 128), BF16),
            pltpu.VMEM((8, 2, 32, 128), BF16),
            pltpu.VMEM((4, 2, 4, 32, 512), BF16),
            pltpu.VMEM((8, 256, 256), BF16),
            pltpu.VMEM((2, 128, 128), BF16),
            pltpu.VMEM((8, 2, 32, 128), BF16),
            pltpu.VMEM((8, 2, 32, 128), BF16),
            pltpu.VMEM((7, 256, 128), BF16),
            pltpu.VMEM((2, 256, 128), BF16),
            pltpu.VMEM((2, 256, 128), BF16),
            pltpu.VMEM((2, 256, 128), BF16),
            pltpu.VMEM((2, 128, 128), BF16),
            pltpu.VMEM((2, 256, 128), F32),
            pltpu.VMEM((8, 32, 128), BF16),
            pltpu.VMEM((8, 32, 128), BF16),
            pltpu.VMEM((4, 128, 512), BF16),
            pltpu.VMEM((4, 128, 512), BF16),
            pltpu.VMEM((4, 128, 512), F32),
            pltpu.VMEM((4, 128, 512), BF16),
            pltpu.VMEM((4, 128, 512), BF16),
            pltpu.VMEM((8, 32, 256), BF16),
            pltpu.VMEM((8, 32, 256), BF16),
            pltpu.VMEM((8, 32, 256), BF16),
            pltpu.VMEM((8, 32, 128), F32),
            sem((8,)), sem((8,)), sem((8,)), sem((8,)),
            sem((4,)), sem((4,)), sem((4,)), sem((4,)), sem((4,)), sem((4,)),
            sem((12,)), sem((12,)), sem((8,)), sem((8,)), sem((8,)), sem((8,)),
            sem((1,)), sem((1,)), sem((4,)), sem((4,)), sem((8,)), sem((8,)),
            sem((8,)), sem((8,)), sem((8,)), sem((8,)), sem((8,)), sem((8,)),
        ],
        compiler_params=pltpu.CompilerParams(
            collective_id=0, has_side_effects=True, vmem_limit_bytes=63 * 1024 * 1024
        ),
    )(volume, depth_kernel, mix_weight, mix_bias.reshape(1, 32), out_grad)
    act, vg, kg, wg, bg = pl.pallas_call(
        finish_kernel,
        out_shape=shapes,
        in_specs=[vmem] * 5,
        out_specs=(hbm,) * 5,
        scratch_shapes=[sem((5,))],
        compiler_params=pltpu.CompilerParams(vmem_limit_bytes=63 * 1024 * 1024),
    )(*results)
    return act, vg, kg, wg, bg.reshape(32)


def solution(mesh):
    placed = (
        P("patch", "chan", None),
        P(None, "chan"),
        P("chan", None),
        P("chan"),
        P("patch", "chan", None),
    )
    return jax.shard_map(
        body,
        mesh=mesh,
        in_specs=placed,
        out_specs=(
            P("patch", "chan", None),
            P("patch", "chan", None),
            P(None, "chan"),
            P("chan", None),
            P("chan"),
        ),
        check_vma=False,
    )
```

```python
import jax
import jax.numpy as jnp
from jax import lax
from jax.experimental import pallas as pl
from jax.experimental.pallas import tpu as pltpu
from jax.sharding import PartitionSpec as P

MESH = pl.DeviceIdType.MESH
F32 = jnp.float32
BF16 = jnp.bfloat16
CELLS = 1024
PLANE = 512
SIDE = 32


def lanes(shape):
    return lax.broadcasted_iota(jnp.int32, shape, len(shape) - 1)


def inside_masks(shape):
    lane = lanes(shape)
    column = lane % SIDE
    row = (lane // SIDE) % 16
    return {
        ("c", 1): column < SIDE - 1,
        ("c", -1): column > 0,
        ("r", 1): row < 15,
        ("r", -1): row > 0,
    }


def moved(values, masks, kind, step):
    if step == 0:
        return values
    amount = step * (1 if kind == "c" else SIDE)
    rolled = pltpu.roll(values, (-amount) % CELLS, 1)
    return jnp.where(masks[(kind, step)], rolled, 0.0)


def tap(a, b, c):
    return 9 * (a + 1) + 3 * (b + 1) + (c + 1)


def kernel(
    vol_hbm, dk_hbm, w_hbm, bias_hbm, og_hbm,
    act_hbm, vg_hbm, kg_hbm, wg_hbm, bg_hbm,
    vol_ref, dk_ref, w_ref, bias_ref, og_ref, act_ref, vg_ref, kg_ref, wg_ref, bg_ref, in_sem, out_sem,
    mst, ogs, g_buf, ogb, wb, wt, pg_ref, apst, apb, pm, r1, r2, r3, r4, mid, mgs, mgr,
    sbs, sbr, cs, xb, xr, zb, zr, fb, kbs,
    m_s, m_r, o_s, o_r, wz_s, wz_r, wx_s, wx_r, wc_s, wc_r, y_s, y_r, ry_s, ry_r, ap_s, ap_r,
    c_s, c_r, x_s, x_r, z_s, z_r, f_s, f_r, b_s, b_r, k_s, k_r,
):
    chan = lax.axis_index("chan")
    patch = lax.axis_index("patch")
    y, i = chan // 8, chan % 8
    zh, core = i // 2, i % 2
    x, zl = patch // 2, patch % 2
    other = 1 - core

    def at_i(r, d):
        return (y * 8 + ((zh + r) % 4) * 2 + (core + d) % 2, patch)

    def at_y(k):
        return (((y + k) % 8) * 8 + i, patch)

    def at_x(k):
        return (chan, ((x + k) % 4) * 2 + zl)

    def at_p(k):
        return (chan, (patch + k) % 8)

    def at_z(r, l):
        return (y * 8 + ((zh + r) % 4) * 2 + core, x * 2 + (zl + l) % 2)

    sibling = at_i(0, 1)
    around = [(2, 0), (2, 1), (1, 0), (3, 0), (1, 1), (3, 1), (0, 1)]

    pending = []

    def send(src, dst, ssem, rsem, where):
        copy = pltpu.make_async_remote_copy(
            src_ref=src, dst_ref=dst, send_sem=ssem, recv_sem=rsem, device_id=where, device_id_type=MESH
        )
        copy.start()
        pending.append(copy)

    def arrive(dst, ssem, rsem, where):
        pltpu.make_async_remote_copy(
            src_ref=dst, dst_ref=dst, send_sem=ssem, recv_sem=rsem, device_id=where, device_id_type=MESH
        ).wait_recv()

    barrier = pltpu.get_barrier_semaphore()
    peers = [at_i(r, d) for r, d in around] + [at_y(k) for k in (1, 2, 6, 7)] + [at_p(k) for k in range(1, 8)]
    peers += [at_z(r, 1) for r in (1, 2, 3)]
    for peer in peers:
        pl.semaphore_signal(barrier, inc=1, device_id=peer, device_id_type=MESH)

    loads = [
        pltpu.make_async_copy(src, dst, in_sem.at[n])
        for n, (src, dst) in enumerate(
            [(vol_hbm, vol_ref), (dk_hbm, dk_ref), (w_hbm, w_ref), (bias_hbm, bias_ref), (og_hbm, og_ref)]
        )
    ]
    for load in loads:
        load.start()
    loads[1].wait()
    loads[0].wait()

    eye = (
        lax.broadcasted_iota(jnp.int32, (27, 128), 0) == lax.broadcasted_iota(jnp.int32, (27, 128), 1)
    ).astype(F32).astype(BF16)
    taps = lax.dot_general(dk_ref[...], eye, (((0,), (0,)), ((), ())), preferred_element_type=F32)

    masks = inside_masks((8, CELLS))
    for g in range(4):
        rows = slice(8 * g, 8 * g + 8)
        v = vol_ref[0, rows, :].astype(F32)
        vc = {c: moved(v, masks, "c", c) for c in (-1, 0, 1)}
        total = None
        for b in (-1, 0, 1):
            def mixed(a, plane):
                part = slice(plane * PLANE, plane * PLANE + PLANE)
                out = None
                for c in (-1, 0, 1):
                    t = tap(a, b, c)
                    term = taps[rows, t : t + 1] * vc[c][:, part]
                    out = term if out is None else out + term
                return out

            first = mixed(0, 0) + mixed(1, 1)
            second = mixed(0, 1) + mixed(-1, 0)
            part = moved(jnp.concatenate([first, second], axis=1), masks, "r", b)
            total = part if total is None else total + part
        for k in range(8):
            mst[k // 2, k % 2, rows, :] = total[:, 128 * k : 128 * k + 128].astype(BF16)

    pl.semaphore_wait(barrier, len(peers))

    for r, d in around:
        send(
            mst.at[(zh + r) % 4, (core + d) % 2], g_buf.at[y, zh, core],
            m_s.at[2 * r + d], m_r.at[2 * r + d], at_i(r, d),
        )
    loads[2].wait()
    quarter = pl.ds(pl.multiple_of(x * 512, 512), 512)
    for r in (2, 1, 3):
        send(w_ref.at[:, quarter], wb.at[x, core, zh], wz_s.at[r], wz_r.at[r], at_z(r, 0))
    wb[x, core, zh] = w_ref[:, quarter]
    g_buf[y, zh, core] = mst[zh, core]

    def weights_on(p):
        piece = wb.at[x, core, (zh + p) % 4]
        for k in (2, 1, 3):
            send(piece, piece, wx_s.at[4 * k + p], wx_r.at[4 * k + p], at_x(k))

    def weights_in(p):
        r = (-p) % 4
        arrive(wb.at[x, core, (zh + p) % 4], wz_s.at[r], wz_r.at[r], at_z(p, 0))
        weights_on(p)

    weights_on(0)

    def block(k, p):
        return g_buf.at[(y + k) % 8, (zh + p) % 4]

    def pass_on(k, p, n, to):
        send(block(k, p), block(k, p), y_s.at[n], y_r.at[n], at_y(to))

    def mixed_in_here(p):
        r = (-p) % 4
        for d in (0, 1):
            if (r, d) != (0, 0):
                arrive(
                    g_buf.at[y, (zh + p) % 4, (core + d) % 2], m_s.at[2 * r + d], m_r.at[2 * r + d], at_i(p, d)
                )
        pass_on(0, p, p, 2)
        pass_on(0, p, 4 + p, 6)

    def forward(p):
        arrive(block(-2, p), y_s.at[p], y_r.at[p], at_y(6))
        if p in (0, 2):
            pass_on(-2, p, 16 + p, 2)
        pass_on(-2, p, 8 + p, 1)
        arrive(block(2, p), y_s.at[4 + p], y_r.at[4 + p], at_y(2))
        if p in (1, 3):
            pass_on(2, p, 16 + p, 6)
        pass_on(2, p, 12 + p, 7)

    mixed_in_here(0)
    loads[3].wait()
    loads[4].wait()
    diag = lax.broadcasted_iota(jnp.int32, (32, 32), 0) == lax.broadcasted_iota(jnp.int32, (32, 32), 1)
    spread = jnp.where(diag, jnp.broadcast_to(bias_ref[...].astype(F32), (32, 32)), 0.0).astype(BF16)
    bias = jnp.dot(spread, jnp.ones((32, 128), BF16), preferred_element_type=F32).astype(BF16)
    for k in range(8):
        ogs[k // 2, k % 2, 0] = og_ref[0, :, 128 * k : 128 * k + 128]
        ogs[k // 2, k % 2, 1] = bias
    ogb[core, zh] = ogs[zh, core]

    mixed_in_here(1)
    mixed_in_here(3)
    weights_in(1)
    weights_in(3)
    mixed_in_here(2)
    for k in (0, 1):
        send(g_buf.at[y], g_buf.at[y], y_s.at[20 + k], y_r.at[20 + k], at_y((1, 7)[k]))
    forward(0)
    weights_in(2)
    for r, d in around:
        send(
            ogs.at[(zh + r) % 4, (core + d) % 2], ogb.at[core, zh], o_s.at[2 * r + d], o_r.at[2 * r + d], at_i(r, d)
        )
    send(wb.at[x, core], wb.at[x, core], wc_s.at[0], wc_r.at[0], sibling)
    forward(1)
    forward(3)
    forward(2)

    for k in (1, 3, 2):
        q = (x - k) % 4
        for p in range(4):
            arrive(wb.at[q, core, (zh + p) % 4], wx_s.at[4 * k + p], wx_r.at[4 * k + p], at_x(4 - k))
        send(wb.at[q, core], wb.at[q, core], wc_s.at[k], wc_r.at[k], sibling)
    for k in (0, 1, 3, 2):
        q = (x - k) % 4
        arrive(wb.at[q, other], wc_s.at[k], wc_r.at[k], sibling)
        part = wb[q].reshape(256, 512)
        for h in range(2):
            wt[2 * q + h] = part[:, 256 * h : 256 * h + 256].T

    for r, d in around:
        arrive(
            ogb.at[(core + d) % 2, (zh - r) % 4], o_s.at[2 * r + d], o_r.at[2 * r + d], at_i(-r, d)
        )
    arrive(g_buf.at[(y - 1) % 8], y_s.at[20], y_r.at[20], at_y(7))
    arrive(g_buf.at[(y + 1) % 8], y_s.at[21], y_r.at[21], at_y(1))
    for p in (0, 1, 3, 2):
        arrive(block(-3, p), y_s.at[8 + p], y_r.at[8 + p], at_y(7))
        arrive(block(3, p), y_s.at[12 + p], y_r.at[12 + p], at_y(1))
        arrive(block(4, p), y_s.at[16 + p], y_r.at[16 + p], at_y(6 if p in (0, 2) else 2))

    def mixed_quarter(q):
        return g_buf[2 * q : 2 * q + 2].reshape(512, 128)

    pre = ogb[:, :, 1].reshape(256, 128).astype(F32)
    for q in range(4):
        pre = pre + jnp.dot(wb[q].reshape(256, 512), mixed_quarter(q), preferred_element_type=F32)
    gate = jax.nn.sigmoid(pre)
    pre_grad = (ogb[:, :, 0].reshape(256, 128).astype(F32) * gate * (1.0 + pre * (1.0 - gate))).astype(BF16)
    pg_ref[...] = pre_grad.reshape(2, 128, 128)

    def partial(k):
        return jnp.dot(wt[(y + k) % 8], pre_grad, preferred_element_type=F32).reshape(4, 64, 128)

    for n, k in enumerate((4, -3, 3, -1, 1)):
        pm[n] = partial(k).astype(BF16)
    far_first = (2, 1, 3, 0)
    for p in far_first:
        at = (zh + p) % 4
        if p in (2, 1):
            send(pm.at[0, at], r4.at[p], ry_s.at[p], ry_r.at[p], at_y(6))
        else:
            send(pm.at[0, at], r4.at[p], ry_s.at[p], ry_r.at[p], at_y(2))
        send(pm.at[1, at], r3.at[0, p], ry_s.at[4 + p], ry_r.at[4 + p], at_y(7))
        send(pm.at[2, at], r3.at[1, p], ry_s.at[8 + p], ry_r.at[8 + p], at_y(1))
        send(pm.at[3, at], r1.at[0, p], ry_s.at[12 + p], ry_r.at[12 + p], at_y(7))
        send(pm.at[4, at], r1.at[1, p], ry_s.at[16 + p], ry_r.at[16 + p], at_y(1))

    theirs = pg_ref[other]
    for k in (2, 1, 3, 0):
        q = (x + k) % 4
        sbs[k] = lax.dot_general(
            theirs, g_buf[pl.ds(2 * q, 2)].reshape(512, 128), (((1,), (1,)), ((), ())), preferred_element_type=F32
        ).astype(BF16)
        send(sbs.at[k], sbr.at[k], c_s.at[k], c_r.at[k], sibling)

    mid[0] = partial(-2)
    mid[1] = partial(2)
    mid[2] = partial(0)
    mine = pg_ref[core]
    for k in (2, 1, 3, 0):
        q = (x + k) % 4
        cs[k] = lax.dot_general(
            mine, g_buf[pl.ds(2 * q, 2)].reshape(512, 128), (((1,), (1,)), ((), ())), preferred_element_type=F32
        )

    for k in (2, 1, 3):
        arrive(sbr.at[k], c_s.at[k], c_r.at[k], sibling)
        xb[k] = (cs[k] + sbr[k].astype(F32)).astype(BF16).reshape(4, 32, 512)
    for p in far_first:
        at = (zh + p) % 4
        for k in (2, 1, 3):
            send(xb.at[k, at], xr.at[k, p], x_s.at[4 * k + p], x_r.at[4 * k + p], at_x(k))

    def add_on_the_way(p):
        at = (zh + p) % 4
        arrive(r3.at[0, p], ry_s.at[4 + p], ry_r.at[4 + p], at_y(1))
        arrive(r3.at[1, p], ry_s.at[8 + p], ry_r.at[8 + p], at_y(7))
        down = mid[0, at] + r3[0, p].astype(F32)
        up = mid[1, at] + r3[1, p].astype(F32)
        if p in (2, 1):
            arrive(r4.at[p], ry_s.at[p], ry_r.at[p], at_y(2))
            down = down + r4[p].astype(F32)
        else:
            arrive(r4.at[p], ry_s.at[p], ry_r.at[p], at_y(6))
            up = up + r4[p].astype(F32)
        pm[5, at] = down.astype(BF16)
        send(pm.at[5, at], r2.at[0, p], ry_s.at[20 + p], ry_r.at[20 + p], at_y(6))
        pm[6, at] = up.astype(BF16)
        send(pm.at[6, at], r2.at[1, p], ry_s.at[24 + p], ry_r.at[24 + p], at_y(2))

    def mixed_grad_here(p):
        at = (zh + p) % 4
        arrive(r1.at[0, p], ry_s.at[12 + p], ry_r.at[12 + p], at_y(1))
        arrive(r1.at[1, p], ry_s.at[16 + p], ry_r.at[16 + p], at_y(7))
        arrive(r2.at[0, p], ry_s.at[20 + p], ry_r.at[20 + p], at_y(2))
        arrive(r2.at[1, p], ry_s.at[24 + p], ry_r.at[24 + p], at_y(6))
        total = mid[2, at] + r1[0, p].astype(F32) + r1[1, p].astype(F32) + r2[0, p].astype(F32) + r2[1, p].astype(F32)
        mgs[at] = total.astype(BF16).reshape(2, 32, 128)
        for d in (0, 1):
            if (p, d) != (0, 0):
                send(
                    mgs.at[at, (core + d) % 2], mgr.at[zh, core], b_s.at[2 * p + d], b_r.at[2 * p + d], at_i(p, d)
                )

    add_on_the_way(2)
    apst[:, :, 0] = (pre * gate).astype(BF16).reshape(2, 4, 32, 128)
    apst[:, :, 1] = pre_grad.reshape(2, 4, 32, 128)
    for r, d in around:
        send(
            apst.at[(core + d) % 2, (zh + r) % 4], apb.at[zh, core], ap_s.at[2 * r + d], ap_r.at[2 * r + d], at_i(r, d)
        )
    apb[zh, core] = apst[core, zh]
    arrive(sbr.at[0], c_s.at[0], c_r.at[0], sibling)
    cs[0] = cs[0] + sbr[0].astype(F32)

    add_on_the_way(1)
    add_on_the_way(3)
    add_on_the_way(0)
    mixed_grad_here(2)

    xs = cs.at[0]

    def weights_grad_on(p):
        at = (zh + p) % 4
        part = xs[pl.ds(pl.multiple_of(32 * at, 32), 32), :]
        for k in (1, 2, 3):
            arrive(xr.at[k, p], x_s.at[4 * k + p], x_r.at[4 * k + p], at_x(4 - k))
            part = part + xr[k, p].astype(F32)
        for l in range(2):
            zb[p, l] = part[:, 256 * l : 256 * l + 256].astype(BF16)
        for l in (0, 1):
            if (p, l) != (0, 0):
                n = 2 * p + l
                send(zb.at[p, (zl + l) % 2], zr.at[n], z_s.at[n], z_r.at[n], at_z(p, l))

    for r, d in around:
        arrive(apb.at[(zh - r) % 4, (core + d) % 2], ap_s.at[2 * r + d], ap_r.at[2 * r + d], at_i(-r, d))
    bias_sum = None
    for k in range(8):
        act_ref[0, :, 128 * k : 128 * k + 128] = apb[k // 2, k % 2, 0]
        part = apb[k // 2, k % 2, 1].astype(F32)
        bias_sum = part if bias_sum is None else bias_sum + part
    bias_sum = jnp.sum(bias_sum, axis=1, keepdims=True)

    results = [
        pltpu.make_async_copy(src, dst, out_sem.at[n])
        for n, (src, dst) in enumerate(
            [(act_ref, act_hbm), (vg_ref, vg_hbm), (kg_ref, kg_hbm), (wg_ref, wg_hbm), (bg_ref, bg_hbm)]
        )
    ]
    results[0].start()

    mixed_grad_here(1)
    mixed_grad_here(3)
    weights_grad_on(2)
    mixed_grad_here(0)
    mgr[zh, core] = mgs[zh, core]
    weights_grad_on(1)
    weights_grad_on(3)

    for r, d in around:
        arrive(mgr.at[(zh - r) % 4, (core + d) % 2], b_s.at[2 * r + d], b_r.at[2 * r + d], at_i(-r, d))

    lane = lanes((8, 128))
    packed = None
    for g in range(4):
        rows = slice(8 * g, 8 * g + 8)
        v = vol_ref[0, rows, :].astype(F32)
        grad = jnp.concatenate([mgr[k // 2, k % 2, rows, :].astype(F32) for k in range(8)], axis=1)
        v0, v1 = v[:, :PLANE], v[:, PLANE:]
        out0 = jnp.zeros((8, PLANE), F32)
        out1 = jnp.zeros((8, PLANE), F32)
        tile = jnp.where(lane == 27, bias_sum[rows, :], 0.0)
        for b in (-1, 0, 1):
            row_moved = moved(grad, masks, "r", -b)
            for c in (-1, 0, 1):
                gm = moved(row_moved, masks, "c", -c)
                g0, g1 = gm[:, :PLANE], gm[:, PLANE:]
                tm, tz, tp = tap(-1, b, c), tap(0, b, c), tap(1, b, c)
                out0 = out0 + taps[rows, tz : tz + 1] * g0 + taps[rows, tm : tm + 1] * g1
                out1 = out1 + taps[rows, tz : tz + 1] * g1 + taps[rows, tp : tp + 1] * g0
                for t, product in ((tm, v0 * g1), (tz, v0 * g0 + v1 * g1), (tp, v1 * g0)):
                    tile = jnp.where(lane == t, jnp.sum(product, axis=1, keepdims=True), tile)
        vg_ref[0, rows, :PLANE] = out0.astype(BF16)
        vg_ref[0, rows, PLANE:] = out1.astype(BF16)
        packed = tile if g == 0 else packed + pltpu.roll(tile, 32 * g, 1)
    kbs[patch] = packed
    for k in (4, 3, 5, 2, 6, 1, 7):
        send(kbs.at[patch], kbs.at[patch], k_s.at[k], k_r.at[k], at_p(k))
    results[1].start()

    weights_grad_on(0)
    final = zb[0, zl].astype(F32)
    for n in (4, 5, 2, 3, 6, 7, 1):
        arrive(zr.at[n], z_s.at[n], z_r.at[n], at_z(-(n // 2), n % 2))
        final = final + zr[n].astype(F32)
    fb[patch] = final.astype(BF16)
    for k in (4, 3, 5, 2, 6, 1, 7):
        send(fb.at[patch], fb.at[patch], f_s.at[k], f_r.at[k], at_p(k))

    for k in range(1, 8):
        arrive(kbs.at[(patch - k) % 8], k_s.at[k], k_r.at[k], at_p(8 - k))
    packed = kbs[0]
    for k in range(1, 8):
        packed = packed + kbs[k]
    turned = jnp.concatenate(
        [packed] + [pltpu.roll(packed, 128 - 32 * g, 1) for g in range(1, 4)], axis=0
    ).T
    kg_ref[...] = turned[:27, :]
    bg_ref[...] = turned[27:28, :]
    results[2].start()
    results[4].start()
    for k in range(1, 8):
        arrive(fb.at[(patch - k) % 8], f_s.at[k], f_r.at[k], at_p(8 - k))
    for k in range(8):
        wg_ref[:, 256 * k : 256 * k + 256] = fb[k].astype(F32)
    results[3].start()
    for copy in pending:
        copy.wait_send()
    for result in results:
        result.wait()


def finish_kernel(*refs):
    sources, results, sems = refs[:5], refs[5:10], refs[10]
    copies = [pltpu.make_async_copy(a, b, sems.at[n]) for n, (a, b) in enumerate(zip(sources, results))]
    for copy in copies:
        copy.start()
    for copy in copies:
        copy.wait()


def body(volume, depth_kernel, mix_weight, mix_bias, out_grad):
    hbm = pl.BlockSpec(memory_space=pltpu.HBM)
    sem = pltpu.SemaphoreType.DMA
    shapes = (
        jax.ShapeDtypeStruct((1, 32, CELLS), BF16),
        jax.ShapeDtypeStruct((1, 32, CELLS), BF16),
        jax.ShapeDtypeStruct((27, 32), F32),
        jax.ShapeDtypeStruct((32, 2048), F32),
        jax.ShapeDtypeStruct((1, 32), F32),
    )
    results = pl.pallas_call(
        kernel,
        out_shape=shapes,
        in_specs=[hbm] * 5,
        out_specs=(hbm,) * 5,
        scratch_shapes=[
            pltpu.VMEM((1, 32, CELLS), BF16),
            pltpu.VMEM((27, 32), BF16),
            pltpu.VMEM((32, 2048), BF16),
            pltpu.VMEM((1, 32), BF16),
            pltpu.VMEM((1, 32, CELLS), BF16),
            pltpu.VMEM((1, 32, CELLS), BF16),
            pltpu.VMEM((1, 32, CELLS), BF16),
            pltpu.VMEM((27, 32), F32),
            pltpu.VMEM((32, 2048), F32),
            pltpu.VMEM((1, 32), F32),
            sem((5,)), sem((5,)),
            pltpu.VMEM((4, 2, 32, 128), BF16),
            pltpu.VMEM((4, 2, 2, 32, 128), BF16),
            pltpu.VMEM((8, 4, 2, 32, 128), BF16),
            pltpu.VMEM((2, 4, 2, 32, 128), BF16),
            pltpu.VMEM((4, 2, 4, 32, 512), BF16),
            pltpu.VMEM((8, 256, 256), BF16),
            pltpu.VMEM((2, 128, 128), BF16),
            pltpu.VMEM((2, 4, 2, 32, 128), BF16),
            pltpu.VMEM((4, 2, 2, 32, 128), BF16),
            pltpu.VMEM((7, 4, 64, 128), BF16),
            pltpu.VMEM((2, 4, 64, 128), BF16),
            pltpu.VMEM((2, 4, 64, 128), BF16),
            pltpu.VMEM((2, 4, 64, 128), BF16),
            pltpu.VMEM((4, 64, 128), BF16),
            pltpu.VMEM((3, 4, 64, 128), F32),
            pltpu.VMEM((4, 2, 32, 128), BF16),
            pltpu.VMEM((4, 2, 32, 128), BF16),
            pltpu.VMEM((4, 128, 512), BF16),
            pltpu.VMEM((4, 128, 512), BF16),
            pltpu.VMEM((4, 128, 512), F32),
            pltpu.VMEM((4, 4, 32, 512), BF16),
            pltpu.VMEM((4, 4, 32, 512), BF16),
            pltpu.VMEM((4, 2, 32, 256), BF16),
            pltpu.VMEM((8, 32, 256), BF16),
            pltpu.VMEM((8, 32, 256), BF16),
            pltpu.VMEM((8, 8, 128), F32),
            sem((8,)), sem((8,)), sem((8,)), sem((8,)),
            sem((4,)), sem((4,)), sem((16,)), sem((16,)), sem((4,)), sem((4,)),
            sem((22,)), sem((22,)), sem((28,)), sem((28,)), sem((8,)), sem((8,)),
            sem((4,)), sem((4,)), sem((16,)), sem((16,)), sem((8,)), sem((8,)),
            sem((8,)), sem((8,)), sem((8,)), sem((8,)), sem((8,)), sem((8,)),
        ],
        compiler_params=pltpu.CompilerParams(
            collective_id=0, has_side_effects=True, vmem_limit_bytes=63 * 1024 * 1024
        ),
    )(volume, depth_kernel, mix_weight, mix_bias.reshape(1, 32), out_grad)
    act, vg, kg, wg, bg = pl.pallas_call(
        finish_kernel,
        out_shape=shapes,
        in_specs=[hbm] * 5,
        out_specs=(hbm,) * 5,
        scratch_shapes=[sem((5,))],
        compiler_params=pltpu.CompilerParams(vmem_limit_bytes=63 * 1024 * 1024),
    )(*results)
    return act, vg, kg, wg, bg.reshape(32)


def solution(mesh):
    placed = (
        P("patch", "chan", None),
        P(None, "chan"),
        P("chan", None),
        P("chan"),
        P("patch", "chan", None),
    )
    return jax.shard_map(
        body,
        mesh=mesh,
        in_specs=placed,
        out_specs=(
            P("patch", "chan", None),
            P("patch", "chan", None),
            P(None, "chan"),
            P("chan", None),
            P("chan"),
        ),
        check_vma=False,
    )
```

```python
import jax
import jax.numpy as jnp
from jax import lax
from jax.experimental import pallas as pl
from jax.experimental.pallas import tpu as pltpu
from jax.sharding import PartitionSpec as P

MESH = pl.DeviceIdType.MESH
F32 = jnp.float32
BF16 = jnp.bfloat16
CELLS = 1024
PLANE = 512
SIDE = 32


def lanes(shape):
    return lax.broadcasted_iota(jnp.int32, shape, len(shape) - 1)


def inside_masks(shape):
    lane = lanes(shape)
    column = lane % SIDE
    row = (lane // SIDE) % 16
    return {
        ("c", 1): column < SIDE - 1,
        ("c", -1): column > 0,
        ("r", 1): row < 15,
        ("r", -1): row > 0,
    }


def moved(values, masks, kind, step):
    if step == 0:
        return values
    amount = step * (1 if kind == "c" else SIDE)
    rolled = pltpu.roll(values, (-amount) % CELLS, 1)
    return jnp.where(masks[(kind, step)], rolled, 0.0)


def tap(a, b, c):
    return 9 * (a + 1) + 3 * (b + 1) + (c + 1)


def kernel(
    vol_hbm, dk_hbm, w_hbm, bias_hbm, og_hbm,
    act_hbm, vg_hbm, kg_hbm, wg_hbm, bg_hbm,
    vol_ref, dk_ref, w_ref, bias_ref, og_ref, act_ref, vg_ref, kg_ref, wg_ref, bg_ref, in_sem, out_sem,
    mst, ogs, g_buf, ogb, wb, wt, pg_ref, apst, apb, pm, r1, r2, r3, r4, mid, mgs, mgr,
    sbs, sbr, cs, xb, xr, zb, zr, fb, kbs,
    m_s, m_r, o_s, o_r, wz_s, wz_r, wx_s, wx_r, wc_s, wc_r, y_s, y_r, ry_s, ry_r, ap_s, ap_r,
    c_s, c_r, x_s, x_r, z_s, z_r, f_s, f_r, b_s, b_r, k_s, k_r,
):
    chan = lax.axis_index("chan")
    patch = lax.axis_index("patch")
    y, i = chan // 8, chan % 8
    zh, core = i // 2, i % 2
    x, zl = patch // 2, patch % 2
    other = 1 - core

    def at_i(r, d):
        return (y * 8 + ((zh + r) % 4) * 2 + (core + d) % 2, patch)

    def at_y(k):
        return (((y + k) % 8) * 8 + i, patch)

    def at_x(k):
        return (chan, ((x + k) % 4) * 2 + zl)

    def at_p(k):
        return (chan, (patch + k) % 8)

    def at_z(r, l):
        return (y * 8 + ((zh + r) % 4) * 2 + core, x * 2 + (zl + l) % 2)

    sibling = at_i(0, 1)
    around = [(2, 0), (2, 1), (1, 0), (3, 0), (1, 1), (3, 1), (0, 1)]

    pending = []

    def send(src, dst, ssem, rsem, where):
        copy = pltpu.make_async_remote_copy(
            src_ref=src, dst_ref=dst, send_sem=ssem, recv_sem=rsem, device_id=where, device_id_type=MESH
        )
        copy.start()
        pending.append(copy)

    def arrive(dst, ssem, rsem, where):
        pltpu.make_async_remote_copy(
            src_ref=dst, dst_ref=dst, send_sem=ssem, recv_sem=rsem, device_id=where, device_id_type=MESH
        ).wait_recv()

    barrier = pltpu.get_barrier_semaphore()
    peers = [at_i(r, d) for r, d in around] + [at_y(k) for k in (1, 2, 6, 7)] + [at_p(k) for k in range(1, 8)]
    peers += [at_z(r, 1) for r in (1, 2, 3)]
    for peer in peers:
        pl.semaphore_signal(barrier, inc=1, device_id=peer, device_id_type=MESH)

    loads = [
        pltpu.make_async_copy(src, dst, in_sem.at[n])
        for n, (src, dst) in enumerate(
            [(vol_hbm, vol_ref), (dk_hbm, dk_ref), (w_hbm, w_ref), (bias_hbm, bias_ref), (og_hbm, og_ref)]
        )
    ]
    for load in loads:
        load.start()
    loads[1].wait()
    loads[0].wait()

    eye = (
        lax.broadcasted_iota(jnp.int32, (27, 128), 0) == lax.broadcasted_iota(jnp.int32, (27, 128), 1)
    ).astype(F32).astype(BF16)
    taps = lax.dot_general(dk_ref[...], eye, (((0,), (0,)), ((), ())), preferred_element_type=F32)

    masks = inside_masks((8, CELLS))
    for g in range(4):
        rows = slice(8 * g, 8 * g + 8)
        v = vol_ref[0, rows, :].astype(F32)
        vc = {c: moved(v, masks, "c", c) for c in (-1, 0, 1)}
        total = None
        for b in (-1, 0, 1):
            def mixed(a, plane):
                part = slice(plane * PLANE, plane * PLANE + PLANE)
                out = None
                for c in (-1, 0, 1):
                    t = tap(a, b, c)
                    term = taps[rows, t : t + 1] * vc[c][:, part]
                    out = term if out is None else out + term
                return out

            first = mixed(0, 0) + mixed(1, 1)
            second = mixed(0, 1) + mixed(-1, 0)
            part = moved(jnp.concatenate([first, second], axis=1), masks, "r", b)
            total = part if total is None else total + part
        for k in range(8):
            mst[k // 2, k % 2, rows, :] = total[:, 128 * k : 128 * k + 128].astype(BF16)

    pl.semaphore_wait(barrier, len(peers))

    for r, d in around:
        send(
            mst.at[(zh + r) % 4, (core + d) % 2], g_buf.at[y, zh, core],
            m_s.at[2 * r + d], m_r.at[2 * r + d], at_i(r, d),
        )
    loads[2].wait()
    quarter = pl.ds(pl.multiple_of(x * 512, 512), 512)
    for r in (2, 1, 3):
        send(w_ref.at[:, quarter], wb.at[x, core, zh], wz_s.at[r], wz_r.at[r], at_z(r, 0))
    wb[x, core, zh] = w_ref[:, quarter]
    g_buf[y, zh, core] = mst[zh, core]

    def weights_on(p):
        piece = wb.at[x, core, (zh + p) % 4]
        for k in (2, 1, 3):
            send(piece, piece, wx_s.at[4 * k + p], wx_r.at[4 * k + p], at_x(k))

    def weights_in(p):
        r = (-p) % 4
        arrive(wb.at[x, core, (zh + p) % 4], wz_s.at[r], wz_r.at[r], at_z(p, 0))
        weights_on(p)

    weights_on(0)

    def block(k, p):
        return g_buf.at[(y + k) % 8, (zh + p) % 4]

    def pass_on(k, p, n, to):
        send(block(k, p), block(k, p), y_s.at[n], y_r.at[n], at_y(to))

    def mixed_in_here(p):
        r = (-p) % 4
        for d in (0, 1):
            if (r, d) != (0, 0):
                arrive(
                    g_buf.at[y, (zh + p) % 4, (core + d) % 2], m_s.at[2 * r + d], m_r.at[2 * r + d], at_i(p, d)
                )
        pass_on(0, p, p, 2)
        pass_on(0, p, 4 + p, 6)

    def forward(p):
        arrive(block(-2, p), y_s.at[p], y_r.at[p], at_y(6))
        if p in (0, 2):
            pass_on(-2, p, 16 + p, 2)
        pass_on(-2, p, 8 + p, 1)
        arrive(block(2, p), y_s.at[4 + p], y_r.at[4 + p], at_y(2))
        if p in (1, 3):
            pass_on(2, p, 16 + p, 6)
        pass_on(2, p, 12 + p, 7)

    mixed_in_here(0)
    loads[3].wait()
    loads[4].wait()
    diag = lax.broadcasted_iota(jnp.int32, (32, 32), 0) == lax.broadcasted_iota(jnp.int32, (32, 32), 1)
    spread = jnp.where(diag, jnp.broadcast_to(bias_ref[...].astype(F32), (32, 32)), 0.0).astype(BF16)
    bias = jnp.dot(spread, jnp.ones((32, 128), BF16), preferred_element_type=F32).astype(BF16)
    for k in range(8):
        ogs[k // 2, k % 2, 0] = og_ref[0, :, 128 * k : 128 * k + 128]
        ogs[k // 2, k % 2, 1] = bias
    ogb[core, zh] = ogs[zh, core]

    mixed_in_here(1)
    mixed_in_here(3)
    weights_in(1)
    weights_in(3)
    mixed_in_here(2)
    for k in (0, 1):
        send(g_buf.at[y], g_buf.at[y], y_s.at[20 + k], y_r.at[20 + k], at_y((1, 7)[k]))
    forward(0)
    weights_in(2)
    for r, d in around:
        send(
            ogs.at[(zh + r) % 4, (core + d) % 2], ogb.at[core, zh], o_s.at[2 * r + d], o_r.at[2 * r + d], at_i(r, d)
        )
    send(wb.at[x, core], wb.at[x, core], wc_s.at[0], wc_r.at[0], sibling)
    forward(1)
    forward(3)
    forward(2)

    for k in (1, 3, 2):
        q = (x - k) % 4
        for p in range(4):
            arrive(wb.at[q, core, (zh + p) % 4], wx_s.at[4 * k + p], wx_r.at[4 * k + p], at_x(4 - k))
        send(wb.at[q, core], wb.at[q, core], wc_s.at[k], wc_r.at[k], sibling)
    for k in (0, 1, 3, 2):
        q = (x - k) % 4
        arrive(wb.at[q, other], wc_s.at[k], wc_r.at[k], sibling)
        part = wb[q].reshape(256, 512)
        for h in range(2):
            wt[2 * q + h] = part[:, 256 * h : 256 * h + 256].T

    for r, d in around:
        arrive(
            ogb.at[(core + d) % 2, (zh - r) % 4], o_s.at[2 * r + d], o_r.at[2 * r + d], at_i(-r, d)
        )
    arrive(g_buf.at[(y - 1) % 8], y_s.at[20], y_r.at[20], at_y(7))
    arrive(g_buf.at[(y + 1) % 8], y_s.at[21], y_r.at[21], at_y(1))
    for p in (0, 1, 3, 2):
        arrive(block(-3, p), y_s.at[8 + p], y_r.at[8 + p], at_y(7))
        arrive(block(3, p), y_s.at[12 + p], y_r.at[12 + p], at_y(1))
        arrive(block(4, p), y_s.at[16 + p], y_r.at[16 + p], at_y(6 if p in (0, 2) else 2))

    def mixed_quarter(q):
        return g_buf[2 * q : 2 * q + 2].reshape(512, 128)

    pre = ogb[:, :, 1].reshape(256, 128).astype(F32)
    for q in range(4):
        pre = pre + jnp.dot(wb[q].reshape(256, 512), mixed_quarter(q), preferred_element_type=F32)
    gate = jax.nn.sigmoid(pre)
    pre_grad = (ogb[:, :, 0].reshape(256, 128).astype(F32) * gate * (1.0 + pre * (1.0 - gate))).astype(BF16)
    pg_ref[...] = pre_grad.reshape(2, 128, 128)

    def partial(k):
        return jnp.dot(wt[(y + k) % 8], pre_grad, preferred_element_type=F32).reshape(4, 64, 128)

    for n, k in enumerate((4, -3, 3, -1, 1)):
        pm[n] = partial(k).astype(BF16)
    far_first = (2, 1, 3, 0)
    for p in far_first:
        at = (zh + p) % 4
        if p in (2, 1):
            send(pm.at[0, at], r4.at[p], ry_s.at[p], ry_r.at[p], at_y(6))
        else:
            send(pm.at[0, at], r4.at[p], ry_s.at[p], ry_r.at[p], at_y(2))
        send(pm.at[1, at], r3.at[0, p], ry_s.at[4 + p], ry_r.at[4 + p], at_y(7))
        send(pm.at[2, at], r3.at[1, p], ry_s.at[8 + p], ry_r.at[8 + p], at_y(1))
        send(pm.at[3, at], r1.at[0, p], ry_s.at[12 + p], ry_r.at[12 + p], at_y(7))
        send(pm.at[4, at], r1.at[1, p], ry_s.at[16 + p], ry_r.at[16 + p], at_y(1))

    theirs = pg_ref[other]
    for k in (2, 1, 3, 0):
        q = (x + k) % 4
        sbs[k] = lax.dot_general(
            theirs, g_buf[pl.ds(2 * q, 2)].reshape(512, 128), (((1,), (1,)), ((), ())), preferred_element_type=F32
        ).astype(BF16)
        send(sbs.at[k], sbr.at[k], c_s.at[k], c_r.at[k], sibling)

    mid[0] = partial(-2)
    mid[1] = partial(2)
    mid[2] = partial(0)
    mine = pg_ref[core]
    for k in (2, 1, 3, 0):
        q = (x + k) % 4
        cs[k] = lax.dot_general(
            mine, g_buf[pl.ds(2 * q, 2)].reshape(512, 128), (((1,), (1,)), ((), ())), preferred_element_type=F32
        )

    for k in (2, 1, 3):
        arrive(sbr.at[k], c_s.at[k], c_r.at[k], sibling)
        xb[k] = (cs[k] + sbr[k].astype(F32)).astype(BF16).reshape(4, 32, 512)
    for p in far_first:
        at = (zh + p) % 4
        for k in (2, 1, 3):
            send(xb.at[k, at], xr.at[k, p], x_s.at[4 * k + p], x_r.at[4 * k + p], at_x(k))

    def add_on_the_way(p):
        at = (zh + p) % 4
        arrive(r3.at[0, p], ry_s.at[4 + p], ry_r.at[4 + p], at_y(1))
        arrive(r3.at[1, p], ry_s.at[8 + p], ry_r.at[8 + p], at_y(7))
        down = mid[0, at] + r3[0, p].astype(F32)
        up = mid[1, at] + r3[1, p].astype(F32)
        if p in (2, 1):
            arrive(r4.at[p], ry_s.at[p], ry_r.at[p], at_y(2))
            down = down + r4[p].astype(F32)
        else:
            arrive(r4.at[p], ry_s.at[p], ry_r.at[p], at_y(6))
            up = up + r4[p].astype(F32)
        pm[5, at] = down.astype(BF16)
        send(pm.at[5, at], r2.at[0, p], ry_s.at[20 + p], ry_r.at[20 + p], at_y(6))
        pm[6, at] = up.astype(BF16)
        send(pm.at[6, at], r2.at[1, p], ry_s.at[24 + p], ry_r.at[24 + p], at_y(2))

    def mixed_grad_here(p):
        at = (zh + p) % 4
        arrive(r1.at[0, p], ry_s.at[12 + p], ry_r.at[12 + p], at_y(1))
        arrive(r1.at[1, p], ry_s.at[16 + p], ry_r.at[16 + p], at_y(7))
        arrive(r2.at[0, p], ry_s.at[20 + p], ry_r.at[20 + p], at_y(2))
        arrive(r2.at[1, p], ry_s.at[24 + p], ry_r.at[24 + p], at_y(6))
        total = mid[2, at] + r1[0, p].astype(F32) + r1[1, p].astype(F32) + r2[0, p].astype(F32) + r2[1, p].astype(F32)
        mgs[at] = total.astype(BF16).reshape(2, 32, 128)
        for d in (0, 1):
            if (p, d) != (0, 0):
                send(
                    mgs.at[at, (core + d) % 2], mgr.at[zh, core], b_s.at[2 * p + d], b_r.at[2 * p + d], at_i(p, d)
                )

    add_on_the_way(2)
    apst[:, :, 0] = (pre * gate).astype(BF16).reshape(2, 4, 32, 128)
    apst[:, :, 1] = pre_grad.reshape(2, 4, 32, 128)
    for r, d in around:
        send(
            apst.at[(core + d) % 2, (zh + r) % 4], apb.at[zh, core], ap_s.at[2 * r + d], ap_r.at[2 * r + d], at_i(r, d)
        )
    apb[zh, core] = apst[core, zh]
    arrive(sbr.at[0], c_s.at[0], c_r.at[0], sibling)
    cs[0] = cs[0] + sbr[0].astype(F32)

    add_on_the_way(1)
    add_on_the_way(3)
    add_on_the_way(0)
    mixed_grad_here(2)

    xs = cs.at[0]

    def weights_grad_on(p):
        at = (zh + p) % 4
        part = xs[pl.ds(pl.multiple_of(32 * at, 32), 32), :]
        for k in (1, 2, 3):
            arrive(xr.at[k, p], x_s.at[4 * k + p], x_r.at[4 * k + p], at_x(4 - k))
            part = part + xr[k, p].astype(F32)
        for l in range(2):
            zb[p, l] = part[:, 256 * l : 256 * l + 256].astype(BF16)
        for l in (0, 1):
            if (p, l) != (0, 0):
                n = 2 * p + l
                send(zb.at[p, (zl + l) % 2], zr.at[n], z_s.at[n], z_r.at[n], at_z(p, l))

    for r, d in around:
        arrive(apb.at[(zh - r) % 4, (core + d) % 2], ap_s.at[2 * r + d], ap_r.at[2 * r + d], at_i(-r, d))
    bias_sum = None
    for k in range(8):
        act_ref[0, :, 128 * k : 128 * k + 128] = apb[k // 2, k % 2, 0]
        part = apb[k // 2, k % 2, 1].astype(F32)
        bias_sum = part if bias_sum is None else bias_sum + part
    bias_sum = jnp.sum(bias_sum, axis=1, keepdims=True)

    results = [
        pltpu.make_async_copy(src, dst, out_sem.at[n])
        for n, (src, dst) in enumerate(
            [(act_ref, act_hbm), (vg_ref, vg_hbm), (kg_ref, kg_hbm), (wg_ref, wg_hbm), (bg_ref, bg_hbm)]
        )
    ]
    results[0].start()

    mixed_grad_here(1)
    mixed_grad_here(3)
    weights_grad_on(2)
    mixed_grad_here(0)
    mgr[zh, core] = mgs[zh, core]
    weights_grad_on(1)
    weights_grad_on(3)

    for r, d in around:
        arrive(mgr.at[(zh - r) % 4, (core + d) % 2], b_s.at[2 * r + d], b_r.at[2 * r + d], at_i(-r, d))

    lane = lanes((8, 128))
    packed = None
    for g in range(4):
        rows = slice(8 * g, 8 * g + 8)
        v = vol_ref[0, rows, :].astype(F32)
        grad = jnp.concatenate([mgr[k // 2, k % 2, rows, :].astype(F32) for k in range(8)], axis=1)
        v0, v1 = v[:, :PLANE], v[:, PLANE:]
        out0 = jnp.zeros((8, PLANE), F32)
        out1 = jnp.zeros((8, PLANE), F32)
        tile = jnp.where(lane == 27, bias_sum[rows, :], 0.0)
        for b in (-1, 0, 1):
            row_moved = moved(grad, masks, "r", -b)
            for c in (-1, 0, 1):
                gm = moved(row_moved, masks, "c", -c)
                g0, g1 = gm[:, :PLANE], gm[:, PLANE:]
                tm, tz, tp = tap(-1, b, c), tap(0, b, c), tap(1, b, c)
                out0 = out0 + taps[rows, tz : tz + 1] * g0 + taps[rows, tm : tm + 1] * g1
                out1 = out1 + taps[rows, tz : tz + 1] * g1 + taps[rows, tp : tp + 1] * g0
                for t, product in ((tm, v0 * g1), (tz, v0 * g0 + v1 * g1), (tp, v1 * g0)):
                    tile = jnp.where(lane == t, jnp.sum(product, axis=1, keepdims=True), tile)
        vg_ref[0, rows, :PLANE] = out0.astype(BF16)
        vg_ref[0, rows, PLANE:] = out1.astype(BF16)
        packed = tile if g == 0 else packed + pltpu.roll(tile, 32 * g, 1)
    kbs[patch] = packed
    for k in (4, 3, 5, 2, 6, 1, 7):
        send(kbs.at[patch], kbs.at[patch], k_s.at[k], k_r.at[k], at_p(k))
    results[1].start()

    weights_grad_on(0)
    final = zb[0, zl].astype(F32)
    for n in (4, 5, 2, 3, 6, 7, 1):
        arrive(zr.at[n], z_s.at[n], z_r.at[n], at_z(-(n // 2), n % 2))
        final = final + zr[n].astype(F32)
    fb[patch] = final.astype(BF16)
    for k in (4, 3, 5, 2, 6, 1, 7):
        send(fb.at[patch], fb.at[patch], f_s.at[k], f_r.at[k], at_p(k))

    for k in range(1, 8):
        arrive(kbs.at[(patch - k) % 8], k_s.at[k], k_r.at[k], at_p(8 - k))
    packed = kbs[0]
    for k in range(1, 8):
        packed = packed + kbs[k]
    turned = jnp.concatenate(
        [packed] + [pltpu.roll(packed, 128 - 32 * g, 1) for g in range(1, 4)], axis=0
    ).T
    kg_ref[...] = turned[:27, :]
    bg_ref[...] = turned[27:28, :]
    results[2].start()
    results[4].start()
    for k in range(1, 8):
        arrive(fb.at[(patch - k) % 8], f_s.at[k], f_r.at[k], at_p(8 - k))
    for k in range(8):
        wg_ref[:, 256 * k : 256 * k + 256] = fb[k].astype(F32)
    results[3].start()
    for copy in pending:
        copy.wait_send()
    for result in results:
        result.wait()


def finish_kernel(*refs):
    sources, results, sems = refs[:5], refs[5:10], refs[10]
    copies = [pltpu.make_async_copy(a, b, sems.at[n]) for n, (a, b) in enumerate(zip(sources, results))]
    for copy in copies:
        copy.start()
    for copy in copies:
        copy.wait()


def body(volume, depth_kernel, mix_weight, mix_bias, out_grad):
    hbm = pl.BlockSpec(memory_space=pltpu.HBM)
    sem = pltpu.SemaphoreType.DMA
    shapes = (
        jax.ShapeDtypeStruct((1, 32, CELLS), BF16),
        jax.ShapeDtypeStruct((1, 32, CELLS), BF16),
        jax.ShapeDtypeStruct((27, 32), F32),
        jax.ShapeDtypeStruct((32, 2048), F32),
        jax.ShapeDtypeStruct((1, 32), F32),
    )
    results = pl.pallas_call(
        kernel,
        out_shape=shapes,
        in_specs=[hbm] * 5,
        out_specs=(hbm,) * 5,
        scratch_shapes=[
            pltpu.VMEM((1, 32, CELLS), BF16),
            pltpu.VMEM((27, 32), BF16),
            pltpu.VMEM((32, 2048), BF16),
            pltpu.VMEM((1, 32), BF16),
            pltpu.VMEM((1, 32, CELLS), BF16),
            pltpu.VMEM((1, 32, CELLS), BF16),
            pltpu.VMEM((1, 32, CELLS), BF16),
            pltpu.VMEM((27, 32), F32),
            pltpu.VMEM((32, 2048), F32),
            pltpu.VMEM((1, 32), F32),
            sem((5,)), sem((5,)),
            pltpu.VMEM((4, 2, 32, 128), BF16),
            pltpu.VMEM((4, 2, 2, 32, 128), BF16),
            pltpu.VMEM((8, 4, 2, 32, 128), BF16),
            pltpu.VMEM((2, 4, 2, 32, 128), BF16),
            pltpu.VMEM((4, 2, 4, 32, 512), BF16),
            pltpu.VMEM((8, 256, 256), BF16),
            pltpu.VMEM((2, 128, 128), BF16),
            pltpu.VMEM((2, 4, 2, 32, 128), BF16),
            pltpu.VMEM((4, 2, 2, 32, 128), BF16),
            pltpu.VMEM((7, 4, 64, 128), BF16),
            pltpu.VMEM((2, 4, 64, 128), BF16),
            pltpu.VMEM((2, 4, 64, 128), BF16),
            pltpu.VMEM((2, 4, 64, 128), BF16),
            pltpu.VMEM((4, 64, 128), BF16),
            pltpu.VMEM((3, 4, 64, 128), F32),
            pltpu.VMEM((4, 2, 32, 128), BF16),
            pltpu.VMEM((4, 2, 32, 128), BF16),
            pltpu.VMEM((4, 128, 512), BF16),
            pltpu.VMEM((4, 128, 512), BF16),
            pltpu.VMEM((4, 128, 512), F32),
            pltpu.VMEM((4, 4, 32, 512), BF16),
            pltpu.VMEM((4, 4, 32, 512), BF16),
            pltpu.VMEM((4, 2, 32, 256), BF16),
            pltpu.VMEM((8, 32, 256), BF16),
            pltpu.VMEM((8, 32, 256), BF16),
            pltpu.VMEM((8, 8, 128), F32),
            sem((8,)), sem((8,)), sem((8,)), sem((8,)),
            sem((4,)), sem((4,)), sem((16,)), sem((16,)), sem((4,)), sem((4,)),
            sem((22,)), sem((22,)), sem((28,)), sem((28,)), sem((8,)), sem((8,)),
            sem((4,)), sem((4,)), sem((16,)), sem((16,)), sem((8,)), sem((8,)),
            sem((8,)), sem((8,)), sem((8,)), sem((8,)), sem((8,)), sem((8,)),
        ],
        compiler_params=pltpu.CompilerParams(
            collective_id=0, has_side_effects=True, vmem_limit_bytes=63 * 1024 * 1024
        ),
    )(volume, depth_kernel, mix_weight, mix_bias.reshape(1, 32), out_grad)
    act, vg, kg, wg, bg = pl.pallas_call(
        finish_kernel,
        out_shape=shapes,
        in_specs=[pl.BlockSpec(memory_space=pltpu.VMEM)] * 5,
        out_specs=(hbm,) * 5,
        scratch_shapes=[sem((5,))],
        compiler_params=pltpu.CompilerParams(vmem_limit_bytes=63 * 1024 * 1024),
    )(*results)
    return act, vg, kg, wg, bg.reshape(32)


def solution(mesh):
    placed = (
        P("patch", "chan", None),
        P(None, "chan"),
        P("chan", None),
        P("chan"),
        P("patch", "chan", None),
    )
    return jax.shard_map(
        body,
        mesh=mesh,
        in_specs=placed,
        out_specs=(
            P("patch", "chan", None),
            P("patch", "chan", None),
            P(None, "chan"),
            P("chan", None),
            P("chan"),
        ),
        check_vma=False,
    )
```

```python
import jax
import jax.numpy as jnp
from jax import lax
from jax.experimental import pallas as pl
from jax.experimental.pallas import tpu as pltpu
from jax.sharding import PartitionSpec as P

MESH = pl.DeviceIdType.MESH
F32 = jnp.float32
BF16 = jnp.bfloat16
CELLS = 1024
PLANE = 512
SIDE = 32


def lanes(shape):
    return lax.broadcasted_iota(jnp.int32, shape, len(shape) - 1)


def inside_masks(shape):
    lane = lanes(shape)
    column = lane % SIDE
    row = (lane // SIDE) % 16
    return {
        ("c", 1): column < SIDE - 1,
        ("c", -1): column > 0,
        ("r", 1): row < 15,
        ("r", -1): row > 0,
    }


def moved(values, masks, kind, step):
    if step == 0:
        return values
    amount = step * (1 if kind == "c" else SIDE)
    rolled = pltpu.roll(values, (-amount) % CELLS, 1)
    return jnp.where(masks[(kind, step)], rolled, 0.0)


def tap(a, b, c):
    return 9 * (a + 1) + 3 * (b + 1) + (c + 1)


def kernel(
    vol_hbm, dk_hbm, w_hbm, bias_hbm, og_hbm,
    act_hbm, vg_hbm, kg_hbm, wg_hbm, bg_hbm,
    vol_ref, dk_ref, w_ref, bias_ref, og_ref, act_ref, vg_ref, kg_ref, wg_ref, bg_ref, in_sem, out_sem,
    mst, ogs, g_buf, ogb, wb, wt, pg_ref, apst, apb, pm, r1, r2, r3, r4, mid, mgs, mgr,
    sbs, sbr, cs, xb, xr, zb, zr, fb, kbs,
    m_s, m_r, o_s, o_r, wz_s, wz_r, wx_s, wx_r, wc_s, wc_r, y_s, y_r, ry_s, ry_r, ap_s, ap_r,
    c_s, c_r, x_s, x_r, z_s, z_r, f_s, f_r, b_s, b_r, k_s, k_r,
):
    chan = lax.axis_index("chan")
    patch = lax.axis_index("patch")
    y, i = chan // 8, chan % 8
    zh, core = i // 2, i % 2
    x, zl = patch // 2, patch % 2
    other = 1 - core

    def at_i(r, d):
        return (y * 8 + ((zh + r) % 4) * 2 + (core + d) % 2, patch)

    def at_y(k):
        return (((y + k) % 8) * 8 + i, patch)

    def at_x(k):
        return (chan, ((x + k) % 4) * 2 + zl)

    def at_p(k):
        return (chan, (patch + k) % 8)

    def at_z(r, l):
        return (y * 8 + ((zh + r) % 4) * 2 + core, x * 2 + (zl + l) % 2)

    sibling = at_i(0, 1)
    around = [(2, 0), (2, 1), (1, 0), (3, 0), (1, 1), (3, 1), (0, 1)]

    pending = []

    def send(src, dst, ssem, rsem, where):
        copy = pltpu.make_async_remote_copy(
            src_ref=src, dst_ref=dst, send_sem=ssem, recv_sem=rsem, device_id=where, device_id_type=MESH
        )
        copy.start()
        pending.append(copy)

    def arrive(dst, ssem, rsem, where):
        pltpu.make_async_remote_copy(
            src_ref=dst, dst_ref=dst, send_sem=ssem, recv_sem=rsem, device_id=where, device_id_type=MESH
        ).wait_recv()

    barrier = pltpu.get_barrier_semaphore()
    peers = [at_i(r, d) for r, d in around] + [at_y(k) for k in (1, 2, 6, 7)] + [at_p(k) for k in range(1, 8)]
    peers += [at_z(r, 1) for r in (1, 2, 3)]
    for peer in peers:
        pl.semaphore_signal(barrier, inc=1, device_id=peer, device_id_type=MESH)

    loads = [
        pltpu.make_async_copy(src, dst, in_sem.at[n])
        for n, (src, dst) in enumerate(
            [(vol_hbm, vol_ref), (dk_hbm, dk_ref), (w_hbm, w_ref), (bias_hbm, bias_ref), (og_hbm, og_ref)]
        )
    ]
    for load in loads:
        load.start()
    loads[1].wait()
    loads[0].wait()

    eye = (
        lax.broadcasted_iota(jnp.int32, (27, 128), 0) == lax.broadcasted_iota(jnp.int32, (27, 128), 1)
    ).astype(F32).astype(BF16)
    taps = lax.dot_general(dk_ref[...], eye, (((0,), (0,)), ((), ())), preferred_element_type=F32)

    masks = inside_masks((8, CELLS))
    for g in range(4):
        rows = slice(8 * g, 8 * g + 8)
        v = vol_ref[0, rows, :].astype(F32)
        vc = {c: moved(v, masks, "c", c) for c in (-1, 0, 1)}
        total = None
        for b in (-1, 0, 1):
            def mixed(a, plane):
                part = slice(plane * PLANE, plane * PLANE + PLANE)
                out = None
                for c in (-1, 0, 1):
                    t = tap(a, b, c)
                    term = taps[rows, t : t + 1] * vc[c][:, part]
                    out = term if out is None else out + term
                return out

            first = mixed(0, 0) + mixed(1, 1)
            second = mixed(0, 1) + mixed(-1, 0)
            part = moved(jnp.concatenate([first, second], axis=1), masks, "r", b)
            total = part if total is None else total + part
        for k in range(8):
            mst[k // 2, k % 2, rows, :] = total[:, 128 * k : 128 * k + 128].astype(BF16)

    pl.semaphore_wait(barrier, len(peers))

    for r, d in around:
        send(
            mst.at[(zh + r) % 4, (core + d) % 2], g_buf.at[y, zh, core],
            m_s.at[2 * r + d], m_r.at[2 * r + d], at_i(r, d),
        )
    loads[2].wait()
    quarter = pl.ds(pl.multiple_of(x * 512, 512), 512)
    for r in (2, 1, 3):
        send(w_ref.at[:, quarter], wb.at[x, core, zh], wz_s.at[r], wz_r.at[r], at_z(r, 0))
    wb[x, core, zh] = w_ref[:, quarter]
    g_buf[y, zh, core] = mst[zh, core]

    def weights_on(p):
        piece = wb.at[x, core, (zh + p) % 4]
        for k in (2, 1, 3):
            send(piece, piece, wx_s.at[4 * k + p], wx_r.at[4 * k + p], at_x(k))

    def weights_in(p):
        r = (-p) % 4
        arrive(wb.at[x, core, (zh + p) % 4], wz_s.at[r], wz_r.at[r], at_z(p, 0))
        weights_on(p)

    weights_on(0)

    def block(k, p):
        return g_buf.at[(y + k) % 8, (zh + p) % 4]

    def pass_on(k, p, n, to):
        send(block(k, p), block(k, p), y_s.at[n], y_r.at[n], at_y(to))

    def mixed_in_here(p):
        r = (-p) % 4
        for d in (0, 1):
            if (r, d) != (0, 0):
                arrive(
                    g_buf.at[y, (zh + p) % 4, (core + d) % 2], m_s.at[2 * r + d], m_r.at[2 * r + d], at_i(p, d)
                )
        pass_on(0, p, p, 2)
        pass_on(0, p, 4 + p, 6)

    def forward(p):
        arrive(block(-2, p), y_s.at[p], y_r.at[p], at_y(6))
        if p in (0, 2):
            pass_on(-2, p, 16 + p, 2)
        pass_on(-2, p, 8 + p, 1)
        arrive(block(2, p), y_s.at[4 + p], y_r.at[4 + p], at_y(2))
        if p in (1, 3):
            pass_on(2, p, 16 + p, 6)
        pass_on(2, p, 12 + p, 7)

    loads[3].wait()
    loads[4].wait()
    diag = lax.broadcasted_iota(jnp.int32, (32, 32), 0) == lax.broadcasted_iota(jnp.int32, (32, 32), 1)
    spread = jnp.where(diag, jnp.broadcast_to(bias_ref[...].astype(F32), (32, 32)), 0.0).astype(BF16)
    bias = jnp.dot(spread, jnp.ones((32, 128), BF16), preferred_element_type=F32).astype(BF16)
    for k in range(8):
        ogs[k // 2, k % 2, 0] = og_ref[0, :, 128 * k : 128 * k + 128]
        ogs[k // 2, k % 2, 1] = bias
    ogb[core, zh] = ogs[zh, core]

    mixed_in_here(0)
    mixed_in_here(1)
    mixed_in_here(3)
    mixed_in_here(2)
    weights_in(1)
    weights_in(3)
    for k in (0, 1):
        send(g_buf.at[y], g_buf.at[y], y_s.at[20 + k], y_r.at[20 + k], at_y((1, 7)[k]))
    forward(0)
    weights_in(2)
    for r, d in around:
        send(
            ogs.at[(zh + r) % 4, (core + d) % 2], ogb.at[core, zh], o_s.at[2 * r + d], o_r.at[2 * r + d], at_i(r, d)
        )
    send(wb.at[x, core], wb.at[x, core], wc_s.at[0], wc_r.at[0], sibling)
    forward(1)
    forward(3)
    forward(2)

    for k in (1, 3, 2):
        q = (x - k) % 4
        for p in range(4):
            arrive(wb.at[q, core, (zh + p) % 4], wx_s.at[4 * k + p], wx_r.at[4 * k + p], at_x(4 - k))
        send(wb.at[q, core], wb.at[q, core], wc_s.at[k], wc_r.at[k], sibling)
    for k in (0, 1, 3, 2):
        q = (x - k) % 4
        arrive(wb.at[q, other], wc_s.at[k], wc_r.at[k], sibling)
        part = wb[q].reshape(256, 512)
        for h in range(2):
            wt[2 * q + h] = part[:, 256 * h : 256 * h + 256].T

    for r, d in around:
        arrive(
            ogb.at[(core + d) % 2, (zh - r) % 4], o_s.at[2 * r + d], o_r.at[2 * r + d], at_i(-r, d)
        )
    arrive(g_buf.at[(y - 1) % 8], y_s.at[20], y_r.at[20], at_y(7))
    arrive(g_buf.at[(y + 1) % 8], y_s.at[21], y_r.at[21], at_y(1))
    for p in (0, 1, 3, 2):
        arrive(block(-3, p), y_s.at[8 + p], y_r.at[8 + p], at_y(7))
        arrive(block(3, p), y_s.at[12 + p], y_r.at[12 + p], at_y(1))
        arrive(block(4, p), y_s.at[16 + p], y_r.at[16 + p], at_y(6 if p in (0, 2) else 2))

    def mixed_quarter(q):
        return g_buf[2 * q : 2 * q + 2].reshape(512, 128)

    pre = ogb[:, :, 1].reshape(256, 128).astype(F32)
    for q in range(4):
        pre = pre + jnp.dot(wb[q].reshape(256, 512), mixed_quarter(q), preferred_element_type=F32)
    gate = jax.nn.sigmoid(pre)
    pre_grad = (ogb[:, :, 0].reshape(256, 128).astype(F32) * gate * (1.0 + pre * (1.0 - gate))).astype(BF16)
    pg_ref[...] = pre_grad.reshape(2, 128, 128)

    def partial(k):
        return jnp.dot(wt[(y + k) % 8], pre_grad, preferred_element_type=F32).reshape(4, 64, 128)

    for n, k in enumerate((4, -3, 3, -1, 1)):
        pm[n] = partial(k).astype(BF16)
    far_first = (2, 1, 3, 0)
    for p in far_first:
        at = (zh + p) % 4
        if p in (2, 1):
            send(pm.at[0, at], r4.at[p], ry_s.at[p], ry_r.at[p], at_y(6))
        else:
            send(pm.at[0, at], r4.at[p], ry_s.at[p], ry_r.at[p], at_y(2))
        send(pm.at[1, at], r3.at[0, p], ry_s.at[4 + p], ry_r.at[4 + p], at_y(7))
        send(pm.at[2, at], r3.at[1, p], ry_s.at[8 + p], ry_r.at[8 + p], at_y(1))
        send(pm.at[3, at], r1.at[0, p], ry_s.at[12 + p], ry_r.at[12 + p], at_y(7))
        send(pm.at[4, at], r1.at[1, p], ry_s.at[16 + p], ry_r.at[16 + p], at_y(1))

    theirs = pg_ref[other]
    for k in (2, 1, 3, 0):
        q = (x + k) % 4
        sbs[k] = lax.dot_general(
            theirs, g_buf[pl.ds(2 * q, 2)].reshape(512, 128), (((1,), (1,)), ((), ())), preferred_element_type=F32
        ).astype(BF16)
        send(sbs.at[k], sbr.at[k], c_s.at[k], c_r.at[k], sibling)

    mid[0] = partial(-2)
    mid[1] = partial(2)
    mid[2] = partial(0)
    mine = pg_ref[core]
    for k in (2, 1, 3, 0):
        q = (x + k) % 4
        cs[k] = lax.dot_general(
            mine, g_buf[pl.ds(2 * q, 2)].reshape(512, 128), (((1,), (1,)), ((), ())), preferred_element_type=F32
        )

    for k in (2, 1, 3):
        arrive(sbr.at[k], c_s.at[k], c_r.at[k], sibling)
        xb[k] = (cs[k] + sbr[k].astype(F32)).astype(BF16).reshape(4, 32, 512)
    for p in far_first:
        at = (zh + p) % 4
        for k in (2, 1, 3):
            send(xb.at[k, at], xr.at[k, p], x_s.at[4 * k + p], x_r.at[4 * k + p], at_x(k))

    def add_on_the_way(p):
        at = (zh + p) % 4
        arrive(r3.at[0, p], ry_s.at[4 + p], ry_r.at[4 + p], at_y(1))
        arrive(r3.at[1, p], ry_s.at[8 + p], ry_r.at[8 + p], at_y(7))
        down = mid[0, at] + r3[0, p].astype(F32)
        up = mid[1, at] + r3[1, p].astype(F32)
        if p in (2, 1):
            arrive(r4.at[p], ry_s.at[p], ry_r.at[p], at_y(2))
            down = down + r4[p].astype(F32)
        else:
            arrive(r4.at[p], ry_s.at[p], ry_r.at[p], at_y(6))
            up = up + r4[p].astype(F32)
        pm[5, at] = down.astype(BF16)
        send(pm.at[5, at], r2.at[0, p], ry_s.at[20 + p], ry_r.at[20 + p], at_y(6))
        pm[6, at] = up.astype(BF16)
        send(pm.at[6, at], r2.at[1, p], ry_s.at[24 + p], ry_r.at[24 + p], at_y(2))

    def mixed_grad_here(p):
        at = (zh + p) % 4
        arrive(r1.at[0, p], ry_s.at[12 + p], ry_r.at[12 + p], at_y(1))
        arrive(r1.at[1, p], ry_s.at[16 + p], ry_r.at[16 + p], at_y(7))
        arrive(r2.at[0, p], ry_s.at[20 + p], ry_r.at[20 + p], at_y(2))
        arrive(r2.at[1, p], ry_s.at[24 + p], ry_r.at[24 + p], at_y(6))
        total = mid[2, at] + r1[0, p].astype(F32) + r1[1, p].astype(F32) + r2[0, p].astype(F32) + r2[1, p].astype(F32)
        mgs[at] = total.astype(BF16).reshape(2, 32, 128)
        for d in (0, 1):
            if (p, d) != (0, 0):
                send(
                    mgs.at[at, (core + d) % 2], mgr.at[zh, core], b_s.at[2 * p + d], b_r.at[2 * p + d], at_i(p, d)
                )

    add_on_the_way(2)
    apst[:, :, 0] = (pre * gate).astype(BF16).reshape(2, 4, 32, 128)
    apst[:, :, 1] = pre_grad.reshape(2, 4, 32, 128)
    for r, d in around:
        send(
            apst.at[(core + d) % 2, (zh + r) % 4], apb.at[zh, core], ap_s.at[2 * r + d], ap_r.at[2 * r + d], at_i(r, d)
        )
    apb[zh, core] = apst[core, zh]
    arrive(sbr.at[0], c_s.at[0], c_r.at[0], sibling)
    cs[0] = cs[0] + sbr[0].astype(F32)

    add_on_the_way(1)
    add_on_the_way(3)
    add_on_the_way(0)
    mixed_grad_here(2)

    xs = cs.at[0]

    def weights_grad_on(p):
        at = (zh + p) % 4
        part = xs[pl.ds(pl.multiple_of(32 * at, 32), 32), :]
        for k in (1, 2, 3):
            arrive(xr.at[k, p], x_s.at[4 * k + p], x_r.at[4 * k + p], at_x(4 - k))
            part = part + xr[k, p].astype(F32)
        for l in range(2):
            zb[p, l] = part[:, 256 * l : 256 * l + 256].astype(BF16)
        for l in (0, 1):
            if (p, l) != (0, 0):
                n = 2 * p + l
                send(zb.at[p, (zl + l) % 2], zr.at[n], z_s.at[n], z_r.at[n], at_z(p, l))

    for r, d in around:
        arrive(apb.at[(zh - r) % 4, (core + d) % 2], ap_s.at[2 * r + d], ap_r.at[2 * r + d], at_i(-r, d))
    bias_sum = None
    for k in range(8):
        act_ref[0, :, 128 * k : 128 * k + 128] = apb[k // 2, k % 2, 0]
        part = apb[k // 2, k % 2, 1].astype(F32)
        bias_sum = part if bias_sum is None else bias_sum + part
    bias_sum = jnp.sum(bias_sum, axis=1, keepdims=True)

    results = [
        pltpu.make_async_copy(src, dst, out_sem.at[n])
        for n, (src, dst) in enumerate(
            [(act_ref, act_hbm), (vg_ref, vg_hbm), (kg_ref, kg_hbm), (wg_ref, wg_hbm), (bg_ref, bg_hbm)]
        )
    ]
    results[0].start()

    mixed_grad_here(1)
    mixed_grad_here(3)
    weights_grad_on(2)
    mixed_grad_here(0)
    mgr[zh, core] = mgs[zh, core]
    weights_grad_on(1)
    weights_grad_on(3)
    weights_grad_on(0)
    final = zb[0, zl].astype(F32)
    for n in (4, 5, 2, 3, 6, 7, 1):
        arrive(zr.at[n], z_s.at[n], z_r.at[n], at_z(-(n // 2), n % 2))
        final = final + zr[n].astype(F32)
    fb[patch] = final.astype(BF16)
    for k in (4, 3, 5, 2, 6, 1, 7):
        send(fb.at[patch], fb.at[patch], f_s.at[k], f_r.at[k], at_p(k))

    for r, d in around:
        arrive(mgr.at[(zh - r) % 4, (core + d) % 2], b_s.at[2 * r + d], b_r.at[2 * r + d], at_i(-r, d))

    lane = lanes((8, 128))
    packed = None
    for g in range(4):
        rows = slice(8 * g, 8 * g + 8)
        v = vol_ref[0, rows, :].astype(F32)
        grad = jnp.concatenate([mgr[k // 2, k % 2, rows, :].astype(F32) for k in range(8)], axis=1)
        v0, v1 = v[:, :PLANE], v[:, PLANE:]
        out0 = jnp.zeros((8, PLANE), F32)
        out1 = jnp.zeros((8, PLANE), F32)
        tile = jnp.where(lane == 27, bias_sum[rows, :], 0.0)
        for b in (-1, 0, 1):
            row_moved = moved(grad, masks, "r", -b)
            for c in (-1, 0, 1):
                gm = moved(row_moved, masks, "c", -c)
                g0, g1 = gm[:, :PLANE], gm[:, PLANE:]
                tm, tz, tp = tap(-1, b, c), tap(0, b, c), tap(1, b, c)
                out0 = out0 + taps[rows, tz : tz + 1] * g0 + taps[rows, tm : tm + 1] * g1
                out1 = out1 + taps[rows, tz : tz + 1] * g1 + taps[rows, tp : tp + 1] * g0
                for t, product in ((tm, v0 * g1), (tz, v0 * g0 + v1 * g1), (tp, v1 * g0)):
                    tile = jnp.where(lane == t, jnp.sum(product, axis=1, keepdims=True), tile)
        vg_ref[0, rows, :PLANE] = out0.astype(BF16)
        vg_ref[0, rows, PLANE:] = out1.astype(BF16)
        packed = tile if g == 0 else packed + pltpu.roll(tile, 32 * g, 1)
    kbs[patch] = packed
    for k in (4, 3, 5, 2, 6, 1, 7):
        send(kbs.at[patch], kbs.at[patch], k_s.at[k], k_r.at[k], at_p(k))
    results[1].start()

    for k in range(1, 8):
        arrive(fb.at[(patch - k) % 8], f_s.at[k], f_r.at[k], at_p(8 - k))
    for k in range(8):
        wg_ref[:, 256 * k : 256 * k + 256] = fb[k].astype(F32)
    results[3].start()
    for k in range(1, 8):
        arrive(kbs.at[(patch - k) % 8], k_s.at[k], k_r.at[k], at_p(8 - k))
    packed = kbs[0]
    for k in range(1, 8):
        packed = packed + kbs[k]
    turned = jnp.concatenate(
        [packed] + [pltpu.roll(packed, 128 - 32 * g, 1) for g in range(1, 4)], axis=0
    ).T
    kg_ref[...] = turned[:27, :]
    bg_ref[...] = turned[27:28, :]
    results[2].start()
    results[4].start()
    for copy in pending:
        copy.wait_send()
    for result in results:
        result.wait()


def finish_kernel(*refs):
    sources, results, sems = refs[:5], refs[5:10], refs[10]
    copies = [pltpu.make_async_copy(a, b, sems.at[n]) for n, (a, b) in enumerate(zip(sources, results))]
    for copy in copies:
        copy.start()
    for copy in copies:
        copy.wait()


def body(volume, depth_kernel, mix_weight, mix_bias, out_grad):
    hbm = pl.BlockSpec(memory_space=pltpu.HBM)
    sem = pltpu.SemaphoreType.DMA
    shapes = (
        jax.ShapeDtypeStruct((1, 32, CELLS), BF16),
        jax.ShapeDtypeStruct((1, 32, CELLS), BF16),
        jax.ShapeDtypeStruct((27, 32), F32),
        jax.ShapeDtypeStruct((32, 2048), F32),
        jax.ShapeDtypeStruct((1, 32), F32),
    )
    results = pl.pallas_call(
        kernel,
        out_shape=shapes,
        in_specs=[hbm] * 5,
        out_specs=(hbm,) * 5,
        scratch_shapes=[
            pltpu.VMEM((1, 32, CELLS), BF16),
            pltpu.VMEM((27, 32), BF16),
            pltpu.VMEM((32, 2048), BF16),
            pltpu.VMEM((1, 32), BF16),
            pltpu.VMEM((1, 32, CELLS), BF16),
            pltpu.VMEM((1, 32, CELLS), BF16),
            pltpu.VMEM((1, 32, CELLS), BF16),
            pltpu.VMEM((27, 32), F32),
            pltpu.VMEM((32, 2048), F32),
            pltpu.VMEM((1, 32), F32),
            sem((5,)), sem((5,)),
            pltpu.VMEM((4, 2, 32, 128), BF16),
            pltpu.VMEM((4, 2, 2, 32, 128), BF16),
            pltpu.VMEM((8, 4, 2, 32, 128), BF16),
            pltpu.VMEM((2, 4, 2, 32, 128), BF16),
            pltpu.VMEM((4, 2, 4, 32, 512), BF16),
            pltpu.VMEM((8, 256, 256), BF16),
            pltpu.VMEM((2, 128, 128), BF16),
            pltpu.VMEM((2, 4, 2, 32, 128), BF16),
            pltpu.VMEM((4, 2, 2, 32, 128), BF16),
            pltpu.VMEM((7, 4, 64, 128), BF16),
            pltpu.VMEM((2, 4, 64, 128), BF16),
            pltpu.VMEM((2, 4, 64, 128), BF16),
            pltpu.VMEM((2, 4, 64, 128), BF16),
            pltpu.VMEM((4, 64, 128), BF16),
            pltpu.VMEM((3, 4, 64, 128), F32),
            pltpu.VMEM((4, 2, 32, 128), BF16),
            pltpu.VMEM((4, 2, 32, 128), BF16),
            pltpu.VMEM((4, 128, 512), BF16),
            pltpu.VMEM((4, 128, 512), BF16),
            pltpu.VMEM((4, 128, 512), F32),
            pltpu.VMEM((4, 4, 32, 512), BF16),
            pltpu.VMEM((4, 4, 32, 512), BF16),
            pltpu.VMEM((4, 2, 32, 256), BF16),
            pltpu.VMEM((8, 32, 256), BF16),
            pltpu.VMEM((8, 32, 256), BF16),
            pltpu.VMEM((8, 8, 128), F32),
            sem((8,)), sem((8,)), sem((8,)), sem((8,)),
            sem((4,)), sem((4,)), sem((16,)), sem((16,)), sem((4,)), sem((4,)),
            sem((22,)), sem((22,)), sem((28,)), sem((28,)), sem((8,)), sem((8,)),
            sem((4,)), sem((4,)), sem((16,)), sem((16,)), sem((8,)), sem((8,)),
            sem((8,)), sem((8,)), sem((8,)), sem((8,)), sem((8,)), sem((8,)),
        ],
        compiler_params=pltpu.CompilerParams(
            collective_id=0, has_side_effects=True, vmem_limit_bytes=63 * 1024 * 1024
        ),
    )(volume, depth_kernel, mix_weight, mix_bias.reshape(1, 32), out_grad)
    act, vg, kg, wg, bg = pl.pallas_call(
        finish_kernel,
        out_shape=shapes,
        in_specs=[pl.BlockSpec(memory_space=pltpu.VMEM)] * 5,
        out_specs=(hbm,) * 5,
        scratch_shapes=[sem((5,))],
        compiler_params=pltpu.CompilerParams(vmem_limit_bytes=63 * 1024 * 1024),
    )(*results)
    return act, vg, kg, wg, bg.reshape(32)


def solution(mesh):
    placed = (
        P("patch", "chan", None),
        P(None, "chan"),
        P("chan", None),
        P("chan"),
        P("patch", "chan", None),
    )
    return jax.shard_map(
        body,
        mesh=mesh,
        in_specs=placed,
        out_specs=(
            P("patch", "chan", None),
            P("patch", "chan", None),
            P(None, "chan"),
            P("chan", None),
            P("chan"),
        ),
        check_vma=False,
    )
```

```python
import jax
import jax.numpy as jnp
from jax import lax
from jax.experimental import pallas as pl
from jax.experimental.pallas import tpu as pltpu
from jax.sharding import PartitionSpec as P

MESH = pl.DeviceIdType.MESH
F32 = jnp.float32
BF16 = jnp.bfloat16
CELLS = 1024
PLANE = 512
SIDE = 32


def lanes(shape):
    return lax.broadcasted_iota(jnp.int32, shape, len(shape) - 1)


def inside_masks(shape):
    lane = lanes(shape)
    column = lane % SIDE
    row = (lane // SIDE) % 16
    return {
        ("c", 1): column < SIDE - 1,
        ("c", -1): column > 0,
        ("r", 1): row < 15,
        ("r", -1): row > 0,
    }


def moved(values, masks, kind, step):
    if step == 0:
        return values
    amount = step * (1 if kind == "c" else SIDE)
    rolled = pltpu.roll(values, (-amount) % CELLS, 1)
    return jnp.where(masks[(kind, step)], rolled, 0.0)


def tap(a, b, c):
    return 9 * (a + 1) + 3 * (b + 1) + (c + 1)


def kernel(
    vol_hbm, dk_hbm, w_hbm, bias_hbm, og_hbm,
    act_hbm, vg_hbm, kg_hbm, wg_hbm, bg_hbm,
    vol_ref, dk_ref, w_ref, bias_ref, og_ref, act_ref, vg_ref, kg_ref, wg_ref, bg_ref, in_sem, out_sem,
    mst, ogs, g_buf, ogb, wb, wt, pg_ref, apst, apb, pm, r1, r2, r3, r4, mid, mgs, mgr,
    sbs, sbr, cs, xb, xr, zb, zr, fb, kbs,
    m_s, m_r, o_s, o_r, wz_s, wz_r, wx_s, wx_r, wc_s, wc_r, y_s, y_r, ry_s, ry_r, ap_s, ap_r,
    c_s, c_r, x_s, x_r, z_s, z_r, f_s, f_r, b_s, b_r, k_s, k_r,
):
    chan = lax.axis_index("chan")
    patch = lax.axis_index("patch")
    y, i = chan // 8, chan % 8
    zh, core = i // 2, i % 2
    x, zl = patch // 2, patch % 2
    other = 1 - core

    def at_i(r, d):
        return (y * 8 + ((zh + r) % 4) * 2 + (core + d) % 2, patch)

    def at_y(k):
        return (((y + k) % 8) * 8 + i, patch)

    def at_x(k):
        return (chan, ((x + k) % 4) * 2 + zl)

    def at_p(k):
        return (chan, (patch + k) % 8)

    def at_z(r, l):
        return (y * 8 + ((zh + r) % 4) * 2 + core, x * 2 + (zl + l) % 2)

    sibling = at_i(0, 1)
    around = [(2, 0), (2, 1), (1, 0), (3, 0), (1, 1), (3, 1), (0, 1)]

    pending = []

    def send(src, dst, ssem, rsem, where):
        copy = pltpu.make_async_remote_copy(
            src_ref=src, dst_ref=dst, send_sem=ssem, recv_sem=rsem, device_id=where, device_id_type=MESH
        )
        copy.start()
        pending.append(copy)

    def arrive(dst, ssem, rsem, where):
        pltpu.make_async_remote_copy(
            src_ref=dst, dst_ref=dst, send_sem=ssem, recv_sem=rsem, device_id=where, device_id_type=MESH
        ).wait_recv()

    barrier = pltpu.get_barrier_semaphore()
    peers = [at_i(r, d) for r, d in around] + [at_y(k) for k in (1, 2, 6, 7)] + [at_p(k) for k in range(1, 8)]
    peers += [at_z(r, 1) for r in (1, 2, 3)]
    for peer in peers:
        pl.semaphore_signal(barrier, inc=1, device_id=peer, device_id_type=MESH)

    loads = [
        pltpu.make_async_copy(src, dst, in_sem.at[n])
        for n, (src, dst) in enumerate(
            [(vol_hbm, vol_ref), (dk_hbm, dk_ref), (w_hbm, w_ref), (bias_hbm, bias_ref), (og_hbm, og_ref)]
        )
    ]
    for load in loads:
        load.start()
    loads[1].wait()
    loads[0].wait()

    eye = (
        lax.broadcasted_iota(jnp.int32, (27, 128), 0) == lax.broadcasted_iota(jnp.int32, (27, 128), 1)
    ).astype(F32).astype(BF16)
    taps = lax.dot_general(dk_ref[...], eye, (((0,), (0,)), ((), ())), preferred_element_type=F32)

    masks = inside_masks((8, CELLS))
    for g in range(4):
        rows = slice(8 * g, 8 * g + 8)
        v = vol_ref[0, rows, :].astype(F32)
        vc = {c: moved(v, masks, "c", c) for c in (-1, 0, 1)}
        total = None
        for b in (-1, 0, 1):
            def mixed(a, plane):
                part = slice(plane * PLANE, plane * PLANE + PLANE)
                out = None
                for c in (-1, 0, 1):
                    t = tap(a, b, c)
                    term = taps[rows, t : t + 1] * vc[c][:, part]
                    out = term if out is None else out + term
                return out

            first = mixed(0, 0) + mixed(1, 1)
            second = mixed(0, 1) + mixed(-1, 0)
            part = moved(jnp.concatenate([first, second], axis=1), masks, "r", b)
            total = part if total is None else total + part
        for k in range(8):
            mst[k // 2, k % 2, rows, :] = total[:, 128 * k : 128 * k + 128].astype(BF16)

    pl.semaphore_wait(barrier, len(peers))

    for r, d in around:
        send(
            mst.at[(zh + r) % 4, (core + d) % 2], g_buf.at[y, zh, core],
            m_s.at[2 * r + d], m_r.at[2 * r + d], at_i(r, d),
        )
    loads[2].wait()
    quarter = pl.ds(pl.multiple_of(x * 512, 512), 512)
    for r in (2, 1, 3):
        send(w_ref.at[:, quarter], wb.at[x, core, zh], wz_s.at[r], wz_r.at[r], at_z(r, 0))
    wb[x, core, zh] = w_ref[:, quarter]
    g_buf[y, zh, core] = mst[zh, core]

    def weights_on(p):
        piece = wb.at[x, core, (zh + p) % 4]
        for k in (2, 1, 3):
            send(piece, piece, wx_s.at[4 * k + p], wx_r.at[4 * k + p], at_x(k))

    def weights_in(p):
        r = (-p) % 4
        arrive(wb.at[x, core, (zh + p) % 4], wz_s.at[r], wz_r.at[r], at_z(p, 0))
        weights_on(p)

    weights_on(0)

    def block(k, p):
        return g_buf.at[(y + k) % 8, (zh + p) % 4]

    def pass_on(k, p, n, to):
        send(block(k, p), block(k, p), y_s.at[n], y_r.at[n], at_y(to))

    def mixed_in_here(p):
        r = (-p) % 4
        for d in (0, 1):
            if (r, d) != (0, 0):
                arrive(
                    g_buf.at[y, (zh + p) % 4, (core + d) % 2], m_s.at[2 * r + d], m_r.at[2 * r + d], at_i(p, d)
                )
        pass_on(0, p, p, 2)
        pass_on(0, p, 4 + p, 6)

    def forward(p):
        arrive(block(-2, p), y_s.at[p], y_r.at[p], at_y(6))
        if p in (0, 2):
            pass_on(-2, p, 16 + p, 2)
        pass_on(-2, p, 8 + p, 1)
        arrive(block(2, p), y_s.at[4 + p], y_r.at[4 + p], at_y(2))
        if p in (1, 3):
            pass_on(2, p, 16 + p, 6)
        pass_on(2, p, 12 + p, 7)

    loads[3].wait()
    loads[4].wait()
    diag = lax.broadcasted_iota(jnp.int32, (32, 32), 0) == lax.broadcasted_iota(jnp.int32, (32, 32), 1)
    spread = jnp.where(diag, jnp.broadcast_to(bias_ref[...].astype(F32), (32, 32)), 0.0).astype(BF16)
    bias = jnp.dot(spread, jnp.ones((32, 128), BF16), preferred_element_type=F32).astype(BF16)
    for k in range(8):
        ogs[k // 2, k % 2, 0] = og_ref[0, :, 128 * k : 128 * k + 128]
        ogs[k // 2, k % 2, 1] = bias
    ogb[core, zh] = ogs[zh, core]

    mixed_in_here(0)
    mixed_in_here(1)
    mixed_in_here(3)
    mixed_in_here(2)
    weights_in(1)
    weights_in(3)
    for k in (0, 1):
        send(g_buf.at[y], g_buf.at[y], y_s.at[20 + k], y_r.at[20 + k], at_y((1, 7)[k]))
    forward(0)
    weights_in(2)
    for r, d in around:
        send(
            ogs.at[(zh + r) % 4, (core + d) % 2], ogb.at[core, zh], o_s.at[2 * r + d], o_r.at[2 * r + d], at_i(r, d)
        )
    send(wb.at[x, core], wb.at[x, core], wc_s.at[0], wc_r.at[0], sibling)
    forward(1)
    forward(3)
    forward(2)

    for k in (1, 3, 2):
        q = (x - k) % 4
        for p in range(4):
            arrive(wb.at[q, core, (zh + p) % 4], wx_s.at[4 * k + p], wx_r.at[4 * k + p], at_x(4 - k))
        send(wb.at[q, core], wb.at[q, core], wc_s.at[k], wc_r.at[k], sibling)
    for k in (0, 1, 3, 2):
        q = (x - k) % 4
        arrive(wb.at[q, other], wc_s.at[k], wc_r.at[k], sibling)
        part = wb[q].reshape(256, 512)
        for h in range(2):
            wt[2 * q + h] = part[:, 256 * h : 256 * h + 256].T

    for r, d in around:
        arrive(
            ogb.at[(core + d) % 2, (zh - r) % 4], o_s.at[2 * r + d], o_r.at[2 * r + d], at_i(-r, d)
        )
    arrive(g_buf.at[(y - 1) % 8], y_s.at[20], y_r.at[20], at_y(7))
    arrive(g_buf.at[(y + 1) % 8], y_s.at[21], y_r.at[21], at_y(1))
    for p in (0, 1, 3, 2):
        arrive(block(-3, p), y_s.at[8 + p], y_r.at[8 + p], at_y(7))
        arrive(block(3, p), y_s.at[12 + p], y_r.at[12 + p], at_y(1))
        arrive(block(4, p), y_s.at[16 + p], y_r.at[16 + p], at_y(6 if p in (0, 2) else 2))

    def mixed_quarter(q):
        return g_buf[2 * q : 2 * q + 2].reshape(512, 128)

    pre = ogb[:, :, 1].reshape(256, 128).astype(F32)
    for q in range(4):
        pre = pre + jnp.dot(wb[q].reshape(256, 512), mixed_quarter(q), preferred_element_type=F32)
    gate = jax.nn.sigmoid(pre)
    pre_grad = (ogb[:, :, 0].reshape(256, 128).astype(F32) * gate * (1.0 + pre * (1.0 - gate))).astype(BF16)
    pg_ref[...] = pre_grad.reshape(2, 128, 128)

    def partial(k):
        return jnp.dot(wt[(y + k) % 8], pre_grad, preferred_element_type=F32).reshape(4, 64, 128)

    for n, k in enumerate((4, -3, 3, -1, 1)):
        pm[n] = partial(k).astype(BF16)
    far_first = (2, 1, 3, 0)
    for p in far_first:
        at = (zh + p) % 4
        if p in (2, 1):
            send(pm.at[0, at], r4.at[p], ry_s.at[p], ry_r.at[p], at_y(6))
        else:
            send(pm.at[0, at], r4.at[p], ry_s.at[p], ry_r.at[p], at_y(2))
        send(pm.at[1, at], r3.at[0, p], ry_s.at[4 + p], ry_r.at[4 + p], at_y(7))
        send(pm.at[2, at], r3.at[1, p], ry_s.at[8 + p], ry_r.at[8 + p], at_y(1))

    def direct(p):
        at = (zh + p) % 4
        send(pm.at[3, at], r1.at[0, p], ry_s.at[12 + p], ry_r.at[12 + p], at_y(7))
        send(pm.at[4, at], r1.at[1, p], ry_s.at[16 + p], ry_r.at[16 + p], at_y(1))

    direct(2)

    apst[:, :, 0] = (pre * gate).astype(BF16).reshape(2, 4, 32, 128)
    apst[:, :, 1] = pre_grad.reshape(2, 4, 32, 128)
    for r, d in around:
        send(
            apst.at[(core + d) % 2, (zh + r) % 4], apb.at[zh, core], ap_s.at[2 * r + d], ap_r.at[2 * r + d], at_i(r, d)
        )
    apb[zh, core] = apst[core, zh]

    theirs = pg_ref[other]
    for k in (2, 1, 3, 0):
        q = (x + k) % 4
        sbs[k] = lax.dot_general(
            theirs, g_buf[pl.ds(2 * q, 2)].reshape(512, 128), (((1,), (1,)), ((), ())), preferred_element_type=F32
        ).astype(BF16)
        send(sbs.at[k], sbr.at[k], c_s.at[k], c_r.at[k], sibling)

    mid[0] = partial(-2)
    mid[1] = partial(2)
    mid[2] = partial(0)
    mine = pg_ref[core]
    for k in (2, 1, 3, 0):
        q = (x + k) % 4
        cs[k] = lax.dot_general(
            mine, g_buf[pl.ds(2 * q, 2)].reshape(512, 128), (((1,), (1,)), ((), ())), preferred_element_type=F32
        )

    for k in (2, 1, 3):
        arrive(sbr.at[k], c_s.at[k], c_r.at[k], sibling)
        xb[k] = (cs[k] + sbr[k].astype(F32)).astype(BF16).reshape(4, 32, 512)
    for p in far_first:
        at = (zh + p) % 4
        for k in (2, 1, 3):
            send(xb.at[k, at], xr.at[k, p], x_s.at[4 * k + p], x_r.at[4 * k + p], at_x(k))

    def add_on_the_way(p):
        at = (zh + p) % 4
        arrive(r3.at[0, p], ry_s.at[4 + p], ry_r.at[4 + p], at_y(1))
        arrive(r3.at[1, p], ry_s.at[8 + p], ry_r.at[8 + p], at_y(7))
        down = mid[0, at] + r3[0, p].astype(F32)
        up = mid[1, at] + r3[1, p].astype(F32)
        if p in (2, 1):
            arrive(r4.at[p], ry_s.at[p], ry_r.at[p], at_y(2))
            down = down + r4[p].astype(F32)
        else:
            arrive(r4.at[p], ry_s.at[p], ry_r.at[p], at_y(6))
            up = up + r4[p].astype(F32)
        pm[5, at] = down.astype(BF16)
        send(pm.at[5, at], r2.at[0, p], ry_s.at[20 + p], ry_r.at[20 + p], at_y(6))
        pm[6, at] = up.astype(BF16)
        send(pm.at[6, at], r2.at[1, p], ry_s.at[24 + p], ry_r.at[24 + p], at_y(2))

    def mixed_grad_here(p):
        at = (zh + p) % 4
        arrive(r1.at[0, p], ry_s.at[12 + p], ry_r.at[12 + p], at_y(1))
        arrive(r1.at[1, p], ry_s.at[16 + p], ry_r.at[16 + p], at_y(7))
        arrive(r2.at[0, p], ry_s.at[20 + p], ry_r.at[20 + p], at_y(2))
        arrive(r2.at[1, p], ry_s.at[24 + p], ry_r.at[24 + p], at_y(6))
        total = mid[2, at] + r1[0, p].astype(F32) + r1[1, p].astype(F32) + r2[0, p].astype(F32) + r2[1, p].astype(F32)
        mgs[at] = total.astype(BF16).reshape(2, 32, 128)
        for d in (0, 1):
            if (p, d) != (0, 0):
                send(
                    mgs.at[at, (core + d) % 2], mgr.at[zh, core], b_s.at[2 * p + d], b_r.at[2 * p + d], at_i(p, d)
                )

    add_on_the_way(2)
    direct(1)
    direct(3)
    arrive(sbr.at[0], c_s.at[0], c_r.at[0], sibling)
    cs[0] = cs[0] + sbr[0].astype(F32)

    add_on_the_way(1)
    add_on_the_way(3)
    direct(0)
    add_on_the_way(0)
    mixed_grad_here(2)

    xs = cs.at[0]

    def weights_grad_on(p):
        at = (zh + p) % 4
        part = xs[pl.ds(pl.multiple_of(32 * at, 32), 32), :]
        for k in (1, 2, 3):
            arrive(xr.at[k, p], x_s.at[4 * k + p], x_r.at[4 * k + p], at_x(4 - k))
            part = part + xr[k, p].astype(F32)
        for l in range(2):
            zb[p, l] = part[:, 256 * l : 256 * l + 256].astype(BF16)
        for l in (0, 1):
            if (p, l) != (0, 0):
                n = 2 * p + l
                send(zb.at[p, (zl + l) % 2], zr.at[n], z_s.at[n], z_r.at[n], at_z(p, l))

    for r, d in around:
        arrive(apb.at[(zh - r) % 4, (core + d) % 2], ap_s.at[2 * r + d], ap_r.at[2 * r + d], at_i(-r, d))
    bias_sum = None
    for k in range(8):
        act_ref[0, :, 128 * k : 128 * k + 128] = apb[k // 2, k % 2, 0]
        part = apb[k // 2, k % 2, 1].astype(F32)
        bias_sum = part if bias_sum is None else bias_sum + part
    bias_sum = jnp.sum(bias_sum, axis=1, keepdims=True)

    results = [
        pltpu.make_async_copy(src, dst, out_sem.at[n])
        for n, (src, dst) in enumerate(
            [(act_ref, act_hbm), (vg_ref, vg_hbm), (kg_ref, kg_hbm), (wg_ref, wg_hbm), (bg_ref, bg_hbm)]
        )
    ]
    results[0].start()

    mixed_grad_here(1)
    mixed_grad_here(3)
    weights_grad_on(2)
    mixed_grad_here(0)
    mgr[zh, core] = mgs[zh, core]
    weights_grad_on(1)
    weights_grad_on(3)
    weights_grad_on(0)
    for r, d in around:
        arrive(mgr.at[(zh - r) % 4, (core + d) % 2], b_s.at[2 * r + d], b_r.at[2 * r + d], at_i(-r, d))

    lane = lanes((8, 128))
    packed = None
    for g in range(4):
        rows = slice(8 * g, 8 * g + 8)
        v = vol_ref[0, rows, :].astype(F32)
        grad = jnp.concatenate([mgr[k // 2, k % 2, rows, :].astype(F32) for k in range(8)], axis=1)
        v0, v1 = v[:, :PLANE], v[:, PLANE:]
        out0 = jnp.zeros((8, PLANE), F32)
        out1 = jnp.zeros((8, PLANE), F32)
        tile = jnp.where(lane == 27, bias_sum[rows, :], 0.0)
        for b in (-1, 0, 1):
            row_moved = moved(grad, masks, "r", -b)
            for c in (-1, 0, 1):
                gm = moved(row_moved, masks, "c", -c)
                g0, g1 = gm[:, :PLANE], gm[:, PLANE:]
                tm, tz, tp = tap(-1, b, c), tap(0, b, c), tap(1, b, c)
                out0 = out0 + taps[rows, tz : tz + 1] * g0 + taps[rows, tm : tm + 1] * g1
                out1 = out1 + taps[rows, tz : tz + 1] * g1 + taps[rows, tp : tp + 1] * g0
                for t, product in ((tm, v0 * g1), (tz, v0 * g0 + v1 * g1), (tp, v1 * g0)):
                    tile = jnp.where(lane == t, jnp.sum(product, axis=1, keepdims=True), tile)
        vg_ref[0, rows, :PLANE] = out0.astype(BF16)
        vg_ref[0, rows, PLANE:] = out1.astype(BF16)
        packed = tile if g == 0 else packed + pltpu.roll(tile, 32 * g, 1)
    kbs[patch] = packed
    for k in (4, 3, 5, 2, 6, 1, 7):
        send(kbs.at[patch], kbs.at[patch], k_s.at[k], k_r.at[k], at_p(k))
    results[1].start()

    final = zb[0, zl].astype(F32)
    for n in (4, 5, 2, 3, 6, 7, 1):
        arrive(zr.at[n], z_s.at[n], z_r.at[n], at_z(-(n // 2), n % 2))
        final = final + zr[n].astype(F32)
    fb[patch] = final.astype(BF16)
    for k in (4, 3, 5, 2, 6, 1, 7):
        send(fb.at[patch], fb.at[patch], f_s.at[k], f_r.at[k], at_p(k))

    for k in range(1, 8):
        arrive(kbs.at[(patch - k) % 8], k_s.at[k], k_r.at[k], at_p(8 - k))
    packed = kbs[0]
    for k in range(1, 8):
        packed = packed + kbs[k]
    turned = jnp.concatenate(
        [packed] + [pltpu.roll(packed, 128 - 32 * g, 1) for g in range(1, 4)], axis=0
    ).T
    kg_ref[...] = turned[:27, :]
    bg_ref[...] = turned[27:28, :]
    results[2].start()
    results[4].start()
    for k in range(1, 8):
        arrive(fb.at[(patch - k) % 8], f_s.at[k], f_r.at[k], at_p(8 - k))
    for k in range(8):
        wg_ref[:, 256 * k : 256 * k + 256] = fb[k].astype(F32)
    results[3].start()
    for copy in pending:
        copy.wait_send()
    for result in results:
        result.wait()


def finish_kernel(*refs):
    sources, results, sems = refs[:5], refs[5:10], refs[10]
    copies = [pltpu.make_async_copy(a, b, sems.at[n]) for n, (a, b) in enumerate(zip(sources, results))]
    for copy in copies:
        copy.start()
    for copy in copies:
        copy.wait()


def body(volume, depth_kernel, mix_weight, mix_bias, out_grad):
    hbm = pl.BlockSpec(memory_space=pltpu.HBM)
    sem = pltpu.SemaphoreType.DMA
    shapes = (
        jax.ShapeDtypeStruct((1, 32, CELLS), BF16),
        jax.ShapeDtypeStruct((1, 32, CELLS), BF16),
        jax.ShapeDtypeStruct((27, 32), F32),
        jax.ShapeDtypeStruct((32, 2048), F32),
        jax.ShapeDtypeStruct((1, 32), F32),
    )
    results = pl.pallas_call(
        kernel,
        out_shape=shapes,
        in_specs=[hbm] * 5,
        out_specs=(hbm,) * 5,
        scratch_shapes=[
            pltpu.VMEM((1, 32, CELLS), BF16),
            pltpu.VMEM((27, 32), BF16),
            pltpu.VMEM((32, 2048), BF16),
            pltpu.VMEM((1, 32), BF16),
            pltpu.VMEM((1, 32, CELLS), BF16),
            pltpu.VMEM((1, 32, CELLS), BF16),
            pltpu.VMEM((1, 32, CELLS), BF16),
            pltpu.VMEM((27, 32), F32),
            pltpu.VMEM((32, 2048), F32),
            pltpu.VMEM((1, 32), F32),
            sem((5,)), sem((5,)),
            pltpu.VMEM((4, 2, 32, 128), BF16),
            pltpu.VMEM((4, 2, 2, 32, 128), BF16),
            pltpu.VMEM((8, 4, 2, 32, 128), BF16),
            pltpu.VMEM((2, 4, 2, 32, 128), BF16),
            pltpu.VMEM((4, 2, 4, 32, 512), BF16),
            pltpu.VMEM((8, 256, 256), BF16),
            pltpu.VMEM((2, 128, 128), BF16),
            pltpu.VMEM((2, 4, 2, 32, 128), BF16),
            pltpu.VMEM((4, 2, 2, 32, 128), BF16),
            pltpu.VMEM((7, 4, 64, 128), BF16),
            pltpu.VMEM((2, 4, 64, 128), BF16),
            pltpu.VMEM((2, 4, 64, 128), BF16),
            pltpu.VMEM((2, 4, 64, 128), BF16),
            pltpu.VMEM((4, 64, 128), BF16),
            pltpu.VMEM((3, 4, 64, 128), F32),
            pltpu.VMEM((4, 2, 32, 128), BF16),
            pltpu.VMEM((4, 2, 32, 128), BF16),
            pltpu.VMEM((4, 128, 512), BF16),
            pltpu.VMEM((4, 128, 512), BF16),
            pltpu.VMEM((4, 128, 512), F32),
            pltpu.VMEM((4, 4, 32, 512), BF16),
            pltpu.VMEM((4, 4, 32, 512), BF16),
            pltpu.VMEM((4, 2, 32, 256), BF16),
            pltpu.VMEM((8, 32, 256), BF16),
            pltpu.VMEM((8, 32, 256), BF16),
            pltpu.VMEM((8, 8, 128), F32),
            sem((8,)), sem((8,)), sem((8,)), sem((8,)),
            sem((4,)), sem((4,)), sem((16,)), sem((16,)), sem((4,)), sem((4,)),
            sem((22,)), sem((22,)), sem((28,)), sem((28,)), sem((8,)), sem((8,)),
            sem((4,)), sem((4,)), sem((16,)), sem((16,)), sem((8,)), sem((8,)),
            sem((8,)), sem((8,)), sem((8,)), sem((8,)), sem((8,)), sem((8,)),
        ],
        compiler_params=pltpu.CompilerParams(
            collective_id=0, has_side_effects=True, vmem_limit_bytes=63 * 1024 * 1024
        ),
    )(volume, depth_kernel, mix_weight, mix_bias.reshape(1, 32), out_grad)
    act, vg, kg, wg, bg = pl.pallas_call(
        finish_kernel,
        out_shape=shapes,
        in_specs=[pl.BlockSpec(memory_space=pltpu.VMEM)] * 5,
        out_specs=(hbm,) * 5,
        scratch_shapes=[sem((5,))],
        compiler_params=pltpu.CompilerParams(vmem_limit_bytes=63 * 1024 * 1024),
    )(*results)
    return act, vg, kg, wg, bg.reshape(32)


def solution(mesh):
    placed = (
        P("patch", "chan", None),
        P(None, "chan"),
        P("chan", None),
        P("chan"),
        P("patch", "chan", None),
    )
    return jax.shard_map(
        body,
        mesh=mesh,
        in_specs=placed,
        out_specs=(
            P("patch", "chan", None),
            P("patch", "chan", None),
            P(None, "chan"),
            P("chan", None),
            P("chan"),
        ),
        check_vma=False,
    )
```

```python
import jax
import jax.numpy as jnp
from jax import lax
from jax.experimental import pallas as pl
from jax.experimental.pallas import tpu as pltpu
from jax.sharding import PartitionSpec as P

MESH = pl.DeviceIdType.MESH
F32 = jnp.float32
BF16 = jnp.bfloat16
CELLS = 1024
PLANE = 512
SIDE = 32


def lanes(shape):
    return lax.broadcasted_iota(jnp.int32, shape, len(shape) - 1)


def inside_masks(shape):
    lane = lanes(shape)
    column = lane % SIDE
    row = (lane // SIDE) % 16
    return {
        ("c", 1): column < SIDE - 1,
        ("c", -1): column > 0,
        ("r", 1): row < 15,
        ("r", -1): row > 0,
    }


def moved(values, masks, kind, step):
    if step == 0:
        return values
    amount = step * (1 if kind == "c" else SIDE)
    rolled = pltpu.roll(values, (-amount) % CELLS, 1)
    return jnp.where(masks[(kind, step)], rolled, 0.0)


def tap(a, b, c):
    return 9 * (a + 1) + 3 * (b + 1) + (c + 1)


def kernel(
    vol_hbm, dk_hbm, w_hbm, bias_hbm, og_hbm,
    act_hbm, vg_hbm, kg_hbm, wg_hbm, bg_hbm,
    vol_ref, dk_ref, w_ref, bias_ref, og_ref, act_ref, vg_ref, kg_ref, wg_ref, bg_ref, in_sem, out_sem,
    mst, ogs, g_buf, ogb, wb, wt, pg_ref, apst, apb, pm, r1, r2, r3, r4, mid, mgs, mgr,
    sbs, sbr, cs, xb, xr, zb, zr, fb, kbs,
    m_s, m_r, o_s, o_r, wz_s, wz_r, wx_s, wx_r, wc_s, wc_r, y_s, y_r, ry_s, ry_r, ap_s, ap_r,
    c_s, c_r, x_s, x_r, z_s, z_r, f_s, f_r, b_s, b_r, k_s, k_r,
):
    chan = lax.axis_index("chan")
    patch = lax.axis_index("patch")
    y, i = chan // 8, chan % 8
    zh, core = i // 2, i % 2
    x, zl = patch // 2, patch % 2
    other = 1 - core

    def at_i(r, d):
        return (y * 8 + ((zh + r) % 4) * 2 + (core + d) % 2, patch)

    def at_y(k):
        return (((y + k) % 8) * 8 + i, patch)

    def at_x(k):
        return (chan, ((x + k) % 4) * 2 + zl)

    def at_p(k):
        return (chan, (patch + k) % 8)

    def at_z(r, l):
        return (y * 8 + ((zh + r) % 4) * 2 + core, x * 2 + (zl + l) % 2)

    sibling = at_i(0, 1)
    around = [(2, 0), (2, 1), (1, 0), (3, 0), (1, 1), (3, 1), (0, 1)]

    pending = []

    def send(src, dst, ssem, rsem, where):
        copy = pltpu.make_async_remote_copy(
            src_ref=src, dst_ref=dst, send_sem=ssem, recv_sem=rsem, device_id=where, device_id_type=MESH
        )
        copy.start()
        pending.append(copy)

    def arrive(dst, ssem, rsem, where):
        pltpu.make_async_remote_copy(
            src_ref=dst, dst_ref=dst, send_sem=ssem, recv_sem=rsem, device_id=where, device_id_type=MESH
        ).wait_recv()

    barrier = pltpu.get_barrier_semaphore()
    peers = [at_i(r, d) for r, d in around] + [at_y(k) for k in (1, 2, 6, 7)] + [at_p(k) for k in range(1, 8)]
    peers += [at_z(r, 1) for r in (1, 2, 3)]
    for peer in peers:
        pl.semaphore_signal(barrier, inc=1, device_id=peer, device_id_type=MESH)

    loads = [
        pltpu.make_async_copy(src, dst, in_sem.at[n])
        for n, (src, dst) in enumerate(
            [(vol_hbm, vol_ref), (dk_hbm, dk_ref), (w_hbm, w_ref), (bias_hbm, bias_ref), (og_hbm, og_ref)]
        )
    ]
    for load in loads:
        load.start()
    loads[1].wait()
    loads[0].wait()

    eye = (
        lax.broadcasted_iota(jnp.int32, (27, 128), 0) == lax.broadcasted_iota(jnp.int32, (27, 128), 1)
    ).astype(F32).astype(BF16)
    taps = lax.dot_general(dk_ref[...], eye, (((0,), (0,)), ((), ())), preferred_element_type=F32)

    masks = inside_masks((8, CELLS))
    for g in range(4):
        rows = slice(8 * g, 8 * g + 8)
        v = vol_ref[0, rows, :].astype(F32)
        vc = {c: moved(v, masks, "c", c) for c in (-1, 0, 1)}
        total = None
        for b in (-1, 0, 1):
            def mixed(a, plane):
                part = slice(plane * PLANE, plane * PLANE + PLANE)
                out = None
                for c in (-1, 0, 1):
                    t = tap(a, b, c)
                    term = taps[rows, t : t + 1] * vc[c][:, part]
                    out = term if out is None else out + term
                return out

            first = mixed(0, 0) + mixed(1, 1)
            second = mixed(0, 1) + mixed(-1, 0)
            part = moved(jnp.concatenate([first, second], axis=1), masks, "r", b)
            total = part if total is None else total + part
        for k in range(8):
            mst[k // 2, k % 2, rows, :] = total[:, 128 * k : 128 * k + 128].astype(BF16)

    pl.semaphore_wait(barrier, len(peers))

    for r, d in around:
        send(
            mst.at[(zh + r) % 4, (core + d) % 2], g_buf.at[y, zh, core],
            m_s.at[2 * r + d], m_r.at[2 * r + d], at_i(r, d),
        )
    loads[2].wait()
    quarter = pl.ds(pl.multiple_of(x * 512, 512), 512)
    for r in (2, 1, 3):
        send(w_ref.at[:, quarter], wb.at[x, core, zh], wz_s.at[r], wz_r.at[r], at_z(r, 0))
    wb[x, core, zh] = w_ref[:, quarter]
    g_buf[y, zh, core] = mst[zh, core]

    def weights_on(p):
        piece = wb.at[x, core, (zh + p) % 4]
        for k in (2, 1, 3):
            send(piece, piece, wx_s.at[4 * k + p], wx_r.at[4 * k + p], at_x(k))

    def weights_in(p):
        r = (-p) % 4
        arrive(wb.at[x, core, (zh + p) % 4], wz_s.at[r], wz_r.at[r], at_z(p, 0))
        weights_on(p)

    weights_on(0)

    def block(k, p):
        return g_buf.at[(y + k) % 8, (zh + p) % 4]

    def pass_on(k, p, n, to):
        send(block(k, p), block(k, p), y_s.at[n], y_r.at[n], at_y(to))

    def mixed_in_here(p):
        r = (-p) % 4
        for d in (0, 1):
            if (r, d) != (0, 0):
                arrive(
                    g_buf.at[y, (zh + p) % 4, (core + d) % 2], m_s.at[2 * r + d], m_r.at[2 * r + d], at_i(p, d)
                )
        pass_on(0, p, p, 2)
        pass_on(0, p, 4 + p, 6)

    def forward(p):
        arrive(block(-2, p), y_s.at[p], y_r.at[p], at_y(6))
        if p in (0, 2):
            pass_on(-2, p, 16 + p, 2)
        pass_on(-2, p, 8 + p, 1)
        arrive(block(2, p), y_s.at[4 + p], y_r.at[4 + p], at_y(2))
        if p in (1, 3):
            pass_on(2, p, 16 + p, 6)
        pass_on(2, p, 12 + p, 7)

    loads[3].wait()
    loads[4].wait()
    diag = lax.broadcasted_iota(jnp.int32, (32, 32), 0) == lax.broadcasted_iota(jnp.int32, (32, 32), 1)
    spread = jnp.where(diag, jnp.broadcast_to(bias_ref[...].astype(F32), (32, 32)), 0.0).astype(BF16)
    bias = jnp.dot(spread, jnp.ones((32, 128), BF16), preferred_element_type=F32).astype(BF16)
    for k in range(8):
        ogs[k // 2, k % 2, 0] = og_ref[0, :, 128 * k : 128 * k + 128]
        ogs[k // 2, k % 2, 1] = bias
    ogb[core, zh] = ogs[zh, core]

    mixed_in_here(0)
    mixed_in_here(1)
    mixed_in_here(3)
    mixed_in_here(2)
    weights_in(1)
    weights_in(3)
    for k in (0, 1):
        send(g_buf.at[y], g_buf.at[y], y_s.at[20 + k], y_r.at[20 + k], at_y((1, 7)[k]))
    forward(0)
    weights_in(2)
    for r, d in around:
        send(
            ogs.at[(zh + r) % 4, (core + d) % 2], ogb.at[core, zh], o_s.at[2 * r + d], o_r.at[2 * r + d], at_i(r, d)
        )
    send(wb.at[x, core], wb.at[x, core], wc_s.at[0], wc_r.at[0], sibling)
    forward(1)
    forward(3)
    forward(2)

    for k in (1, 3, 2):
        q = (x - k) % 4
        for p in range(4):
            arrive(wb.at[q, core, (zh + p) % 4], wx_s.at[4 * k + p], wx_r.at[4 * k + p], at_x(4 - k))
        send(wb.at[q, core], wb.at[q, core], wc_s.at[k], wc_r.at[k], sibling)
    for k in (0, 1, 3, 2):
        q = (x - k) % 4
        arrive(wb.at[q, other], wc_s.at[k], wc_r.at[k], sibling)
        part = wb[q].reshape(256, 512)
        for h in range(2):
            wt[2 * q + h] = part[:, 256 * h : 256 * h + 256].T

    for r, d in around:
        arrive(
            ogb.at[(core + d) % 2, (zh - r) % 4], o_s.at[2 * r + d], o_r.at[2 * r + d], at_i(-r, d)
        )
    arrive(g_buf.at[(y - 1) % 8], y_s.at[20], y_r.at[20], at_y(7))
    arrive(g_buf.at[(y + 1) % 8], y_s.at[21], y_r.at[21], at_y(1))
    for p in (0, 1, 3, 2):
        arrive(block(-3, p), y_s.at[8 + p], y_r.at[8 + p], at_y(7))
        arrive(block(3, p), y_s.at[12 + p], y_r.at[12 + p], at_y(1))
        arrive(block(4, p), y_s.at[16 + p], y_r.at[16 + p], at_y(6 if p in (0, 2) else 2))

    def mixed_quarter(q):
        return g_buf[2 * q : 2 * q + 2].reshape(512, 128)

    pre = ogb[:, :, 1].reshape(256, 128).astype(F32)
    for q in range(4):
        pre = pre + jnp.dot(wb[q].reshape(256, 512), mixed_quarter(q), preferred_element_type=F32)
    gate = jax.nn.sigmoid(pre)
    pre_grad = (ogb[:, :, 0].reshape(256, 128).astype(F32) * gate * (1.0 + pre * (1.0 - gate))).astype(BF16)
    pg_ref[...] = pre_grad.reshape(2, 128, 128)

    def partial(k):
        return jnp.dot(wt[(y + k) % 8], pre_grad, preferred_element_type=F32).reshape(4, 64, 128)

    for n, k in enumerate((4, -3, 3, -1, 1)):
        pm[n] = partial(k).astype(BF16)
    far_first = (2, 1, 3, 0)
    for p in far_first:
        at = (zh + p) % 4
        if p in (2, 1):
            send(pm.at[0, at], r4.at[p], ry_s.at[p], ry_r.at[p], at_y(6))
        else:
            send(pm.at[0, at], r4.at[p], ry_s.at[p], ry_r.at[p], at_y(2))
        send(pm.at[1, at], r3.at[0, p], ry_s.at[4 + p], ry_r.at[4 + p], at_y(7))
        send(pm.at[2, at], r3.at[1, p], ry_s.at[8 + p], ry_r.at[8 + p], at_y(1))

    def direct(p):
        at = (zh + p) % 4
        send(pm.at[3, at], r1.at[0, p], ry_s.at[12 + p], ry_r.at[12 + p], at_y(7))
        send(pm.at[4, at], r1.at[1, p], ry_s.at[16 + p], ry_r.at[16 + p], at_y(1))

    direct(2)

    apst[:, :, 0] = (pre * gate).astype(BF16).reshape(2, 4, 32, 128)
    apst[:, :, 1] = pre_grad.reshape(2, 4, 32, 128)
    for r, d in around:
        send(
            apst.at[(core + d) % 2, (zh + r) % 4], apb.at[zh, core], ap_s.at[2 * r + d], ap_r.at[2 * r + d], at_i(r, d)
        )
    apb[zh, core] = apst[core, zh]

    theirs = pg_ref[other]
    for k in (2, 1, 3, 0):
        q = (x + k) % 4
        sbs[k] = lax.dot_general(
            theirs, g_buf[pl.ds(2 * q, 2)].reshape(512, 128), (((1,), (1,)), ((), ())), preferred_element_type=F32
        ).astype(BF16)
        send(sbs.at[k], sbr.at[k], c_s.at[k], c_r.at[k], sibling)

    mid[0] = partial(-2)
    mid[1] = partial(2)
    mid[2] = partial(0)
    mine = pg_ref[core]
    for k in (2, 1, 3, 0):
        q = (x + k) % 4
        cs[k] = lax.dot_general(
            mine, g_buf[pl.ds(2 * q, 2)].reshape(512, 128), (((1,), (1,)), ((), ())), preferred_element_type=F32
        )

    for k in (2, 1, 3):
        arrive(sbr.at[k], c_s.at[k], c_r.at[k], sibling)
        xb[k] = (cs[k] + sbr[k].astype(F32)).astype(BF16).reshape(4, 32, 512)
    for p in far_first:
        at = (zh + p) % 4
        for k in (2, 1, 3):
            send(xb.at[k, at], xr.at[k, p], x_s.at[4 * k + p], x_r.at[4 * k + p], at_x(k))

    def add_on_the_way(p):
        at = (zh + p) % 4
        arrive(r3.at[0, p], ry_s.at[4 + p], ry_r.at[4 + p], at_y(1))
        arrive(r3.at[1, p], ry_s.at[8 + p], ry_r.at[8 + p], at_y(7))
        down = mid[0, at] + r3[0, p].astype(F32)
        up = mid[1, at] + r3[1, p].astype(F32)
        if p in (2, 1):
            arrive(r4.at[p], ry_s.at[p], ry_r.at[p], at_y(2))
            down = down + r4[p].astype(F32)
        else:
            arrive(r4.at[p], ry_s.at[p], ry_r.at[p], at_y(6))
            up = up + r4[p].astype(F32)
        pm[5, at] = down.astype(BF16)
        send(pm.at[5, at], r2.at[0, p], ry_s.at[20 + p], ry_r.at[20 + p], at_y(6))
        pm[6, at] = up.astype(BF16)
        send(pm.at[6, at], r2.at[1, p], ry_s.at[24 + p], ry_r.at[24 + p], at_y(2))

    def mixed_grad_here(p):
        at = (zh + p) % 4
        arrive(r1.at[0, p], ry_s.at[12 + p], ry_r.at[12 + p], at_y(1))
        arrive(r1.at[1, p], ry_s.at[16 + p], ry_r.at[16 + p], at_y(7))
        arrive(r2.at[0, p], ry_s.at[20 + p], ry_r.at[20 + p], at_y(2))
        arrive(r2.at[1, p], ry_s.at[24 + p], ry_r.at[24 + p], at_y(6))
        total = mid[2, at] + r1[0, p].astype(F32) + r1[1, p].astype(F32) + r2[0, p].astype(F32) + r2[1, p].astype(F32)
        mgs[at] = total.astype(BF16).reshape(2, 32, 128)
        for d in (0, 1):
            if (p, d) != (0, 0):
                send(
                    mgs.at[at, (core + d) % 2], mgr.at[zh, core], b_s.at[2 * p + d], b_r.at[2 * p + d], at_i(p, d)
                )

    add_on_the_way(2)
    direct(1)
    direct(3)
    arrive(sbr.at[0], c_s.at[0], c_r.at[0], sibling)
    cs[0] = cs[0] + sbr[0].astype(F32)

    add_on_the_way(1)
    add_on_the_way(3)
    direct(0)
    add_on_the_way(0)
    mixed_grad_here(2)

    xs = cs.at[0]

    def weights_grad_on(p):
        at = (zh + p) % 4
        part = xs[pl.ds(pl.multiple_of(32 * at, 32), 32), :]
        for k in (1, 2, 3):
            arrive(xr.at[k, p], x_s.at[4 * k + p], x_r.at[4 * k + p], at_x(4 - k))
            part = part + xr[k, p].astype(F32)
        for l in range(2):
            zb[p, l] = part[:, 256 * l : 256 * l + 256].astype(BF16)
        for l in (0, 1):
            if (p, l) != (0, 0):
                n = 2 * p + l
                send(zb.at[p, (zl + l) % 2], zr.at[n], z_s.at[n], z_r.at[n], at_z(p, l))

    for r, d in around:
        arrive(apb.at[(zh - r) % 4, (core + d) % 2], ap_s.at[2 * r + d], ap_r.at[2 * r + d], at_i(-r, d))
    bias_sum = None
    for k in range(8):
        act_ref[0, :, 128 * k : 128 * k + 128] = apb[k // 2, k % 2, 0]
        part = apb[k // 2, k % 2, 1].astype(F32)
        bias_sum = part if bias_sum is None else bias_sum + part
    bias_sum = jnp.sum(bias_sum, axis=1, keepdims=True)

    results = [
        pltpu.make_async_copy(src, dst, out_sem.at[n])
        for n, (src, dst) in enumerate(
            [(act_ref, act_hbm), (vg_ref, vg_hbm), (kg_ref, kg_hbm), (bg_ref, bg_hbm)]
        )
    ]
    results[0].start()

    mixed_grad_here(1)
    mixed_grad_here(3)
    weights_grad_on(2)
    mixed_grad_here(0)
    mgr[zh, core] = mgs[zh, core]
    weights_grad_on(1)
    weights_grad_on(3)
    weights_grad_on(0)
    for r, d in around:
        arrive(mgr.at[(zh - r) % 4, (core + d) % 2], b_s.at[2 * r + d], b_r.at[2 * r + d], at_i(-r, d))

    lane = lanes((8, 128))
    packed = None
    for g in range(4):
        rows = slice(8 * g, 8 * g + 8)
        v = vol_ref[0, rows, :].astype(F32)
        grad = jnp.concatenate([mgr[k // 2, k % 2, rows, :].astype(F32) for k in range(8)], axis=1)
        v0, v1 = v[:, :PLANE], v[:, PLANE:]
        out0 = jnp.zeros((8, PLANE), F32)
        out1 = jnp.zeros((8, PLANE), F32)
        tile = jnp.where(lane == 27, bias_sum[rows, :], 0.0)
        for b in (-1, 0, 1):
            row_moved = moved(grad, masks, "r", -b)
            for c in (-1, 0, 1):
                gm = moved(row_moved, masks, "c", -c)
                g0, g1 = gm[:, :PLANE], gm[:, PLANE:]
                tm, tz, tp = tap(-1, b, c), tap(0, b, c), tap(1, b, c)
                out0 = out0 + taps[rows, tz : tz + 1] * g0 + taps[rows, tm : tm + 1] * g1
                out1 = out1 + taps[rows, tz : tz + 1] * g1 + taps[rows, tp : tp + 1] * g0
                for t, product in ((tm, v0 * g1), (tz, v0 * g0 + v1 * g1), (tp, v1 * g0)):
                    tile = jnp.where(lane == t, jnp.sum(product, axis=1, keepdims=True), tile)
        vg_ref[0, rows, :PLANE] = out0.astype(BF16)
        vg_ref[0, rows, PLANE:] = out1.astype(BF16)
        packed = tile if g == 0 else packed + pltpu.roll(tile, 32 * g, 1)
    kbs[patch] = packed
    for k in (4, 3, 5, 2, 6, 1, 7):
        send(kbs.at[patch], kbs.at[patch], k_s.at[k], k_r.at[k], at_p(k))
    results[1].start()

    final = zb[0, zl].astype(F32)
    for n in (4, 5, 2, 3, 6, 7, 1):
        arrive(zr.at[n], z_s.at[n], z_r.at[n], at_z(-(n // 2), n % 2))
        final = final + zr[n].astype(F32)
    fb[patch] = final.astype(BF16)
    for k in (4, 3, 5, 2, 6, 1, 7):
        send(fb.at[patch], fb.at[patch], f_s.at[k], f_r.at[k], at_p(k))

    for k in range(1, 8):
        arrive(kbs.at[(patch - k) % 8], k_s.at[k], k_r.at[k], at_p(8 - k))
    packed = kbs[0]
    for k in range(1, 8):
        packed = packed + kbs[k]
    turned = jnp.concatenate(
        [packed] + [pltpu.roll(packed, 128 - 32 * g, 1) for g in range(1, 4)], axis=0
    ).T
    kg_ref[...] = turned[:27, :]
    bg_ref[...] = turned[27:28, :]
    results[2].start()
    results[3].start()
    for k in (0, 1, 7, 2, 6, 3, 5, 4):
        slot = (patch - k) % 8
        if k:
            arrive(fb.at[slot], f_s.at[k], f_r.at[k], at_p(8 - k))
        part = pl.ds(pl.multiple_of(256 * slot, 256), 256)
        wg_ref[:, part] = fb[slot].astype(F32)
        results.append(pltpu.make_async_copy(wg_ref.at[:, part], wg_hbm.at[:, part], out_sem.at[4 + k]))
        results[-1].start()
    for copy in pending:
        copy.wait_send()
    for result in results:
        result.wait()


def finish_kernel(*refs):
    sources, results, sems = refs[:5], refs[5:10], refs[10]
    copies = [pltpu.make_async_copy(a, b, sems.at[n]) for n, (a, b) in enumerate(zip(sources, results))]
    for copy in copies:
        copy.start()
    for copy in copies:
        copy.wait()


def body(volume, depth_kernel, mix_weight, mix_bias, out_grad):
    hbm = pl.BlockSpec(memory_space=pltpu.HBM)
    sem = pltpu.SemaphoreType.DMA
    shapes = (
        jax.ShapeDtypeStruct((1, 32, CELLS), BF16),
        jax.ShapeDtypeStruct((1, 32, CELLS), BF16),
        jax.ShapeDtypeStruct((27, 32), F32),
        jax.ShapeDtypeStruct((32, 2048), F32),
        jax.ShapeDtypeStruct((1, 32), F32),
    )
    results = pl.pallas_call(
        kernel,
        out_shape=shapes,
        in_specs=[hbm] * 5,
        out_specs=(hbm,) * 5,
        scratch_shapes=[
            pltpu.VMEM((1, 32, CELLS), BF16),
            pltpu.VMEM((27, 32), BF16),
            pltpu.VMEM((32, 2048), BF16),
            pltpu.VMEM((1, 32), BF16),
            pltpu.VMEM((1, 32, CELLS), BF16),
            pltpu.VMEM((1, 32, CELLS), BF16),
            pltpu.VMEM((1, 32, CELLS), BF16),
            pltpu.VMEM((27, 32), F32),
            pltpu.VMEM((32, 2048), F32),
            pltpu.VMEM((1, 32), F32),
            sem((5,)), sem((12,)),
            pltpu.VMEM((4, 2, 32, 128), BF16),
            pltpu.VMEM((4, 2, 2, 32, 128), BF16),
            pltpu.VMEM((8, 4, 2, 32, 128), BF16),
            pltpu.VMEM((2, 4, 2, 32, 128), BF16),
            pltpu.VMEM((4, 2, 4, 32, 512), BF16),
            pltpu.VMEM((8, 256, 256), BF16),
            pltpu.VMEM((2, 128, 128), BF16),
            pltpu.VMEM((2, 4, 2, 32, 128), BF16),
            pltpu.VMEM((4, 2, 2, 32, 128), BF16),
            pltpu.VMEM((7, 4, 64, 128), BF16),
            pltpu.VMEM((2, 4, 64, 128), BF16),
            pltpu.VMEM((2, 4, 64, 128), BF16),
            pltpu.VMEM((2, 4, 64, 128), BF16),
            pltpu.VMEM((4, 64, 128), BF16),
            pltpu.VMEM((3, 4, 64, 128), F32),
            pltpu.VMEM((4, 2, 32, 128), BF16),
            pltpu.VMEM((4, 2, 32, 128), BF16),
            pltpu.VMEM((4, 128, 512), BF16),
            pltpu.VMEM((4, 128, 512), BF16),
            pltpu.VMEM((4, 128, 512), F32),
            pltpu.VMEM((4, 4, 32, 512), BF16),
            pltpu.VMEM((4, 4, 32, 512), BF16),
            pltpu.VMEM((4, 2, 32, 256), BF16),
            pltpu.VMEM((8, 32, 256), BF16),
            pltpu.VMEM((8, 32, 256), BF16),
            pltpu.VMEM((8, 8, 128), F32),
            sem((8,)), sem((8,)), sem((8,)), sem((8,)),
            sem((4,)), sem((4,)), sem((16,)), sem((16,)), sem((4,)), sem((4,)),
            sem((22,)), sem((22,)), sem((28,)), sem((28,)), sem((8,)), sem((8,)),
            sem((4,)), sem((4,)), sem((16,)), sem((16,)), sem((8,)), sem((8,)),
            sem((8,)), sem((8,)), sem((8,)), sem((8,)), sem((8,)), sem((8,)),
        ],
        compiler_params=pltpu.CompilerParams(
            collective_id=0, has_side_effects=True, vmem_limit_bytes=63 * 1024 * 1024
        ),
    )(volume, depth_kernel, mix_weight, mix_bias.reshape(1, 32), out_grad)
    act, vg, kg, wg, bg = pl.pallas_call(
        finish_kernel,
        out_shape=shapes,
        in_specs=[pl.BlockSpec(memory_space=pltpu.VMEM)] * 5,
        out_specs=(hbm,) * 5,
        scratch_shapes=[sem((5,))],
        compiler_params=pltpu.CompilerParams(vmem_limit_bytes=63 * 1024 * 1024),
    )(*results)
    return act, vg, kg, wg, bg.reshape(32)


def solution(mesh):
    placed = (
        P("patch", "chan", None),
        P(None, "chan"),
        P("chan", None),
        P("chan"),
        P("patch", "chan", None),
    )
    return jax.shard_map(
        body,
        mesh=mesh,
        in_specs=placed,
        out_specs=(
            P("patch", "chan", None),
            P("patch", "chan", None),
            P(None, "chan"),
            P("chan", None),
            P("chan"),
        ),
        check_vma=False,
    )
```
